32 devices in a mesh: groups: 2 (over y), video: 4 (over x, core), frame: 4 (over z).
Axes of the slice: x: 2, y: 2, z: 4, core: 2. Of those that a mesh axis runs over, the one named last changes fastest.
Arguments:
- latents: bfloat16 [8, 4, 256, 320], P(('groups', 'video'), 'frame'), parts along dimension 0, may hold values from -6 to 6
- timesteps: int32 [8], P(('groups', 'video')), parts along dimension 0, may hold values from 0 to 999
- matchings: int32 [2, 8], P(None, 'groups'), parts along dimension 1, may hold values from 0 to 3, each once within a row
- tile_mask: int32 [2, 8, 2, 2], P(None, 'groups'), parts along dimension 1, may hold values from 0 to 1, as said below
- conv_first: bfloat16 [3, 3, 320, 320], replicated, may hold values from -0.109375 to 0.109375
- conv_second: bfloat16 [3, 3, 320, 320], replicated, may hold values from -0.109375 to 0.109375
- time_proj: bfloat16 [1280, 320], P('frame'), may hold values from -0.15625 to 0.15625
- epi_in: bfloat16 [3, 320, 320], P(None, 'frame'), may hold values from -48 to 48
- epi_out: bfloat16 [320, 320], P('frame'), may hold values from -0.3125 to 0.3125
- temp_in: bfloat16 [3, 320, 320], P(None, 'frame'), may hold values from -48 to 48
- temp_out: bfloat16 [320, 320], P('frame'), may hold values from -0.3125 to 0.3125
Outputs:
- denoised: bfloat16 [8, 4, 256, 320], P(('groups', 'video'), 'frame'), parts along dimension 0
The draws below stay inside these ranges and needn't reach their ends.
There are 2 independent parts, one for each index of `groups`. The reference program is written for one: setup_inputs(seed, part) draws one part's arguments, and reference() takes and returns one part's arrays. A program takes and returns all parts, laid end to end along the dimension named above; an argument that names none is the same for every part. Nothing has to cross between parts.
Inputs may be any that keep to these rules, and one draw needn't show every extreme that they name: Every row tile_mask[m, u, i, :] holds at least one 1.
All inputs are finite; a program needn't handle non-finite values.
Results may differ from the reference program's by a relative error of at most 0.035.
Values may be sent and summed in bfloat16 or wider, within the bound.
A program may use at most 64 MiB of HBM per device.

```python
import math
import jax
import jax.numpy as jnp
from jax import lax

C = 320
HEADS = 8
NORM_GROUPS = 32
TEMB = 1280
H = 8
W = 32
TOKENS = 256
TILES = 2
VIDEOS = 4
FRAMES = 4


def draw_tile_mask(key, part):
    first_key, second_key = jax.random.split(jax.random.fold_in(key, 21))
    random_bits = jax.random.randint(first_key, (2, VIDEOS, TILES, TILES), 0, 2)
    forced = jax.random.randint(second_key, (2, VIDEOS, TILES, 1), 0, TILES)
    columns = jnp.arange(TILES, dtype=jnp.int32)
    return jnp.maximum(random_bits, (columns == forced).astype(jnp.int32)).astype(jnp.int32)


def projection_draw(key):
    base = jax.random.normal(key, (3, C, C), jnp.float32)
    base = jnp.clip(base, -6.0, 6.0) / jnp.sqrt(jnp.float32(C))
    boost = jnp.full((C,), 1.5, jnp.float32)
    factor = jnp.stack([boost, jnp.ones((C,), jnp.float32), jnp.ones((C,), jnp.float32)])
    return jnp.clip(base * factor[:, None, :], -48.0, 48.0).astype(jnp.bfloat16)


def draw_epi_in(key, part):
    return projection_draw(jax.random.fold_in(key, 11))


def draw_temp_in(key, part):
    return projection_draw(jax.random.fold_in(key, 12))


def set_ends(array, key, least, largest):
    extent = array.shape
    index_at = [jax.random.randint(jax.random.fold_in(key, axis), (), 0, extent[axis]) for axis in range(len(extent))]
    array = array.at[tuple(index_at)].set(least)
    longest = extent.index(max(extent))
    index_at[longest] = (index_at[longest] + 1) % extent[longest]
    return array.at[tuple(index_at)].set(largest)


def levels(key, extent, cuts, smallest, high):
    def one(position, parts):
        steps = jax.random.uniform(jax.random.fold_in(jax.random.fold_in(key, 6), position), (parts,), jnp.float32, smallest / len(cuts), high / len(cuts))
        return jnp.repeat(jnp.exp(steps), extent[position] // parts).reshape((-1,) + (1,) * (len(extent) - position - 1))

    factor_of = one(*cuts[0])
    for cut in cuts[1:]:
        factor_of = factor_of * one(*cut)
    return factor_of


def normal_values(stream_key, extent, scale, reach, pieces=(), kind=jnp.bfloat16):
    drawn = jax.random.normal(stream_key, extent, jnp.float32) * scale
    if len(pieces) > 0:
        drawn = levels(stream_key, extent, pieces, -0.22, 0.18) * drawn
    return jnp.clip(drawn, min=-reach, max=reach).astype(kind)


def setup_inputs(seed: int = 0, part: int = 0) -> dict:
    keys = jax.random.split(jax.random.key(seed), 12)
    own_keys = jax.random.split(jax.random.fold_in(keys[11], part), 12)
    return {
        "latents": normal_values(own_keys[0], (VIDEOS, FRAMES, TOKENS, C), 1.0, 6.0, ((0, 4), (1, 4))),
        "timesteps": set_ends(jax.random.randint(own_keys[1], (VIDEOS,), 0, 1000), jax.random.fold_in(own_keys[1], 1), 0, 999).astype(jnp.int32),
        "matchings": jax.vmap(lambda own: jax.random.permutation(own, VIDEOS))(jax.random.split(own_keys[2], 2)).reshape((2, VIDEOS)).astype(jnp.int32),
        "tile_mask": draw_tile_mask(jax.random.fold_in(jax.random.fold_in(keys[11], part), 71), part),
        "conv_first": normal_values(keys[4], (3, 3, C, C), (9 * C) ** -0.5, 0.109375),
        "conv_second": normal_values(keys[5], (3, 3, C, C), (9 * C) ** -0.5, 0.109375),
        "time_proj": normal_values(keys[6], (TEMB, C), TEMB ** -0.5, 0.15625, ((0, 4),)),
        "epi_in": draw_epi_in(jax.random.fold_in(keys[11], 71), part),
        "epi_out": normal_values(keys[8], (C, C), C ** -0.5, 0.3125, ((0, 4),)),
        "temp_in": draw_temp_in(jax.random.fold_in(keys[11], 71), part),
        "temp_out": normal_values(keys[10], (C, C), C ** -0.5, 0.3125, ((0, 4),)),
    }


epsilon = 1e-05
masked_fill = -1e+30

def group_norm(values):
    row_count, channels = values.shape
    grouped = values.reshape(row_count, NORM_GROUPS, channels // NORM_GROUPS)
    average = lax.optimization_barrier(jnp.mean(grouped, axis=(0, 2), keepdims=True))
    spread = lax.optimization_barrier(jnp.mean(jnp.square(grouped - average), axis=(0, 2), keepdims=True))
    return ((grouped - average) / jnp.sqrt(spread + epsilon)).reshape(row_count, channels)

def layer_norm(values):
    average = lax.optimization_barrier(jnp.mean(values, axis=-1, keepdims=True))
    spread = lax.optimization_barrier(jnp.mean(jnp.square(values - average), axis=-1, keepdims=True))
    return (values - average) / jnp.sqrt(spread + epsilon)

def convolve(activations, weight):
    channels = activations.shape[-1]
    planar = activations.reshape(H, W, channels)
    padded = jnp.pad(planar, ((1, 1), (1, 1), (0, 0)))
    totals = jnp.zeros((H * W, weight.shape[-1]), jnp.float32)
    for row_shift in range(3):
        for col_shift in range(3):
            window = padded[row_shift:row_shift + H, col_shift:col_shift + W].reshape(H * W, channels)
            totals = totals + jnp.dot(window, weight[row_shift, col_shift], preferred_element_type=jnp.float32)
    return totals

def sinusoid(timestep):
    half_width = TEMB // 2
    frequency = jnp.exp(-math.log(10000.0) * jnp.arange(half_width, dtype=jnp.float32) / half_width)
    angles = timestep.astype(jnp.float32)[:, None] * frequency[None, :]
    return jnp.concatenate([jnp.cos(angles), jnp.sin(angles)], axis=-1)

def softmax_last(scores):
    maxima = lax.optimization_barrier(jnp.max(scores, axis=-1, keepdims=True))
    powers = jnp.exp(scores - maxima)
    return powers / lax.optimization_barrier(jnp.sum(powers, axis=-1, keepdims=True))

def epipolar(queries, key_rows, value_rows, pair_mask):
    row_count, channels = queries.shape
    tiles = pair_mask.shape[0]
    width = row_count // tiles
    split = (row_count, HEADS, channels // HEADS)
    scaling = 1.0 / math.sqrt(channels // HEADS)
    scores = jnp.einsum('qhd,khd->hqk', queries.reshape(split).astype(jnp.float32), key_rows.reshape(split).astype(jnp.float32)) * scaling
    scores = scores.reshape(HEADS, tiles, width, tiles, width)
    scores = jnp.where(pair_mask[None, :, None, :, None] > 0, scores, masked_fill)
    weights = softmax_last(scores.reshape(HEADS, row_count, row_count)).astype(jnp.bfloat16)
    result = jnp.einsum('hqk,khd->qhd', weights.astype(jnp.float32), value_rows.reshape(split).astype(jnp.float32))
    return result.reshape(row_count, channels)

def frame_attention(queries, key_rows, value_rows):
    frames, pixels, channels = queries.shape
    split = (frames, pixels, HEADS, channels // HEADS)
    scaling = 1.0 / math.sqrt(channels // HEADS)
    scores = jnp.einsum('fphd,gphd->phfg', queries.reshape(split).astype(jnp.float32), key_rows.reshape(split).astype(jnp.float32)) * scaling
    weights = softmax_last(scores).astype(jnp.bfloat16)
    result = jnp.einsum('phfg,gphd->fphd', weights.astype(jnp.float32), value_rows.reshape(split).astype(jnp.float32))
    return result.astype(jnp.bfloat16).reshape(frames, pixels, channels)

def reference(latents, timesteps, matchings, tile_mask, conv_first, conv_second, time_proj, epi_in, epi_out, temp_in, temp_out):
    videos, frames = (latents.shape[0], latents.shape[1])
    time_act = jax.nn.silu(sinusoid(timesteps)).astype(jnp.bfloat16)
    time_bias = jnp.dot(time_act, time_proj, preferred_element_type=jnp.float32)
    bias_rows = jnp.repeat(time_bias, frames, axis=0)
    source_maps = latents.reshape(videos * frames, TOKENS, C)

    def residual_block(item):
        source, bias_row = item
        first_act = jax.nn.silu(group_norm(source.astype(jnp.float32))).astype(jnp.bfloat16)
        inner_sum = convolve(first_act, conv_first) + bias_row[None, :]
        second_act = jax.nn.silu(group_norm(inner_sum)).astype(jnp.bfloat16)
        hidden = (source.astype(jnp.float32) + convolve(second_act, conv_second)).astype(jnp.bfloat16)
        normed = layer_norm(hidden.astype(jnp.float32)).astype(jnp.bfloat16)
        return (hidden, normed)
    hidden, normed = lax.map(residual_block, (source_maps, bias_rows))
    normed_grid = normed.reshape(videos, frames, TOKENS, C)
    matched = jnp.stack([normed_grid[matchings[0]], normed_grid[matchings[1]]], axis=2).reshape(videos * frames, 2, TOKENS, C)
    pair_masks = jnp.repeat(jnp.transpose(tile_mask, (1, 0, 2, 3)), frames, axis=0)

    def cross_view(item):
        own_normed, own_hidden, pair_maps, masks_here = item
        queries = jnp.dot(own_normed, epi_in[0], preferred_element_type=jnp.float32).astype(jnp.bfloat16)
        summed = jnp.zeros((TOKENS, C), jnp.float32)
        for matching in range(2):
            key_rows = jnp.dot(pair_maps[matching], epi_in[1], preferred_element_type=jnp.float32).astype(jnp.bfloat16)
            value_rows = jnp.dot(pair_maps[matching], epi_in[2], preferred_element_type=jnp.float32).astype(jnp.bfloat16)
            summed = summed + epipolar(queries, key_rows, value_rows, masks_here[matching])
        mixture = summed.astype(jnp.bfloat16)
        return (own_hidden.astype(jnp.float32) + jnp.dot(mixture, epi_out, preferred_element_type=jnp.float32)).astype(jnp.bfloat16)
    second_hidden = lax.map(cross_view, (normed, hidden, matched, pair_masks)).reshape(videos, frames, TOKENS, C)

    def temporal(video_maps):
        flat_rows = video_maps.reshape(frames * TOKENS, C)
        temp_normed = layer_norm(flat_rows.astype(jnp.float32)).astype(jnp.bfloat16)
        frame_q = jnp.dot(temp_normed, temp_in[0], preferred_element_type=jnp.float32).astype(jnp.bfloat16).reshape(frames, TOKENS, C)
        frame_k = jnp.dot(temp_normed, temp_in[1], preferred_element_type=jnp.float32).astype(jnp.bfloat16).reshape(frames, TOKENS, C)
        frame_v = jnp.dot(temp_normed, temp_in[2], preferred_element_type=jnp.float32).astype(jnp.bfloat16).reshape(frames, TOKENS, C)
        attended = frame_attention(frame_q, frame_k, frame_v).reshape(frames * TOKENS, C)
        result = flat_rows.astype(jnp.float32) + jnp.dot(attended, temp_out, preferred_element_type=jnp.float32)
        return result.astype(jnp.bfloat16).reshape(frames, TOKENS, C)
    return lax.map(temporal, second_hidden)
```

```python
import functools
import math

import jax
import jax.numpy as jnp
from jax import lax
from jax.experimental import pallas as pl
from jax.experimental.pallas import tpu as pltpu
from jax.sharding import PartitionSpec as P

HEADS = 8
NORM_GROUPS = 32
TEMB = 1280
H = 8
W = 32
EPS = 1e-05
FILL = -1e30
F32 = jnp.float32
BF16 = jnp.bfloat16
MESH = pl.DeviceIdType.MESH


def dot(a, b):
    return jnp.dot(a, b, preferred_element_type=F32)


def dot_nt(a, b):
    return lax.dot_general(a, b, (((1,), (1,)), ((), ())), preferred_element_type=F32)


def iota(shape, dim):
    return lax.broadcasted_iota(jnp.int32, shape, dim)


def split_rows(row):
    hi = row.astype(BF16).astype(F32)
    rest = row - hi
    mid = rest.astype(BF16).astype(F32)
    low = rest - mid
    which = iota((16, row.shape[1]), 0)
    packed = jnp.where(which == 0, hi, jnp.where(which == 1, mid, jnp.where(which == 2, low, 0.0)))
    return packed.astype(BF16)


def group_total(row, same_group):
    return jnp.sum(dot(split_rows(row), same_group), axis=0, keepdims=True)


def gn_silu(values, same_group, count):
    average = group_total(jnp.sum(values, axis=0, keepdims=True), same_group) * (1.0 / count)
    centered = values - average
    spread = group_total(jnp.sum(centered * centered, axis=0, keepdims=True), same_group) * (
        1.0 / count
    )
    u = centered * (1.0 / jnp.sqrt(spread + EPS))
    return u * (1.0 / (1.0 + jnp.exp(-u)))


def layer_norm(values):
    average = jnp.mean(values, axis=-1, keepdims=True)
    centered = values - average
    spread = jnp.mean(centered * centered, axis=-1, keepdims=True)
    return centered * (1.0 / jnp.sqrt(spread + EPS))


def wave(angle, quarter_shift):
    n = jnp.floor(angle * (2.0 / math.pi) + 0.5)
    r = ((angle - n * 1.5703125) - n * 4.837512969970703125e-4) - n * 7.54978995489188216e-8
    z = r * r
    sin_r = r + r * z * (
        -1.6666654611e-1 + z * (8.3321608736e-3 + z * -1.9515295891e-4)
    )
    cos_r = (
        1.0
        - 0.5 * z
        + z * z * (4.166664568298827e-2 + z * (-1.388731625493765e-3 + z * 2.443315711809948e-5))
    )
    q = n + quarter_shift
    q = q - 4.0 * jnp.floor(q * 0.25)
    return jnp.where(
        q < 0.5, cos_r, jnp.where(q < 1.5, -sin_r, jnp.where(q < 2.5, -cos_r, sin_r))
    )


def kernel(
    frames,
    videos,
    chunks,
    steps_ref,
    match_ref,
    mask_ref,
    x_hbm,
    conv_a_hbm,
    conv_b_hbm,
    time_hbm,
    epi_in_hbm,
    epi_out_hbm,
    temp_in_hbm,
    temp_out_hbm,
    out_ref,
    x_ref,
    conv_a,
    conv_b,
    time_w,
    time_parts,
    weights,
    padded,
    hidden_ref,
    normed,
    keys_ref,
    values_ref,
    second_ref,
    send_blocks,
    recv_blocks,
    back_blocks,
    final_blocks,
    local_sem,
    time_send,
    time_recv,
    chain_send,
    chain_recv,
    pair_send,
    pair_recv,
    near_send,
    near_recv,
    far_send,
    far_recv,
    relay_send,
    relay_recv,
    go_send,
    go_recv,
    ret_send,
    ret_recv,
):
    tokens, channels = x_ref.shape
    head_width = channels // HEADS
    frame = lax.axis_index("frame")
    video = lax.axis_index("video")
    core = lax.rem(video, 2)
    column = video // 2
    columns = videos // 2
    partner = column * 2 + (1 - core)
    last = frames - 1

    def video_at(shift, which):
        return lax.rem(column + shift, columns) * 2 + which

    barrier = pltpu.get_barrier_semaphore()
    for d in range(1, frames):
        pl.semaphore_signal(
            barrier, inc=1, device_id={"frame": lax.rem(frame + d, frames)}, device_id_type=MESH
        )
    pl.semaphore_signal(barrier, inc=1, device_id={"video": partner}, device_id_type=MESH)
    for d in range(1, columns):
        pl.semaphore_signal(
            barrier, inc=1, device_id={"video": video_at(d, core)}, device_id_type=MESH
        )

    local = [
        (time_hbm, time_w),
        (epi_in_hbm, weights.at[0, frame, pl.ds(0, 3)]),
        (epi_out_hbm, weights.at[0, frame, 3]),
        (x_hbm.at[0, 0], x_ref),
        (conv_a_hbm, conv_a),
        (conv_b_hbm, conv_b),
        (temp_in_hbm, weights.at[1, frame, pl.ds(0, 3)]),
        (temp_out_hbm, weights.at[1, frame, 3]),
    ]
    local = [pltpu.make_async_copy(a, b, local_sem.at[i]) for i, (a, b) in enumerate(local)]
    for copy in local:
        copy.start()
    pl.semaphore_wait(barrier, frames + columns - 1)

    def remote(src, dst, send, recv, **where):
        return pltpu.make_async_remote_copy(
            src_ref=src,
            dst_ref=dst,
            send_sem=send,
            recv_sem=recv,
            device_id=where,
            device_id_type=MESH,
        )

    mine = pl.ds(core * 2, 2)

    def owner(direction, k):
        return frame - k if direction == 0 else frame + k

    def has(direction, k):
        return frame >= k if direction == 0 else frame + k <= last

    def can_pass(direction):
        return frame < last if direction == 0 else frame > 0

    def chain_copy(s, direction, k):
        block = weights.at[s, owner(direction, k), mine]
        to = frame + 1 if direction == 0 else frame - 1
        return remote(
            block, block, chain_send.at[s, direction, k], chain_recv.at[s, direction, k], frame=to
        )

    def pair_copy(s, direction, k):
        block = weights.at[s, owner(direction, k), mine]
        return remote(
            block, block, pair_send.at[s, direction, k], pair_recv.at[s, direction, k], video=partner
        )

    def chain_step(s, k):
        for direction in range(2):
            if k > 0:

                @pl.when(has(direction, k))
                def _():
                    chain_copy_recv(s, direction, k - 1)
                    pair_copy(s, direction, k).start()

            if k < last:

                @pl.when(jnp.logical_and(has(direction, k), can_pass(direction)))
                def _():
                    chain_copy(s, direction, k).start()

    def chain_copy_recv(s, direction, k):
        block = weights.at[s, owner(direction, k + 1), mine]
        remote(
            block, block, chain_send.at[s, direction, k], chain_recv.at[s, direction, k], frame=frame
        ).wait_recv()

    def chain_finish(s):
        other = pl.ds((1 - core) * 2, 2)
        for direction in range(2):
            for k in range(1, frames):

                @pl.when(has(direction, k))
                def _():
                    block = weights.at[s, owner(direction, k), other]
                    remote(
                        block,
                        block,
                        pair_send.at[s, direction, k],
                        pair_recv.at[s, direction, k],
                        video=partner,
                    ).wait_recv()

    def chain_drain(s):
        for direction in range(2):
            for k in range(frames):
                if k > 0:

                    @pl.when(has(direction, k))
                    def _():
                        pair_copy(s, direction, k).wait_send()

                if k < last:

                    @pl.when(jnp.logical_and(has(direction, k), can_pass(direction)))
                    def _():
                        chain_copy(s, direction, k).wait_send()

    def matrix(s, index):
        return jnp.concatenate([weights[s, f, index] for f in range(frames)], axis=0)

    local[0].wait()
    rows = time_w.shape[0]
    place = iota((16, rows), 1) + frame * rows
    is_sin = place >= TEMB // 2
    index = jnp.where(is_sin, place - TEMB // 2, place).astype(F32)
    frequency = jnp.exp(-math.log(10000.0) * index / (TEMB // 2))
    angle = frequency * steps_ref[0].astype(F32)
    basis = wave(angle, jnp.where(is_sin, 3.0, 0.0))
    time_act = (basis * (1.0 / (1.0 + jnp.exp(-basis)))).astype(BF16)
    time_parts[0] = dot(time_act, time_w[...])[0:8]

    def time_copy(d):
        return remote(
            time_parts.at[0],
            time_parts.at[d],
            time_send.at[d - 1],
            time_recv.at[d - 1],
            frame=lax.rem(frame + d, frames),
        )

    for d in range(1, frames):
        time_copy(d).start()
    local[1].wait()
    local[2].wait()
    chain_step(0, 0)

    group_width = channels // NORM_GROUPS
    row_group = jnp.floor((iota((channels, channels), 0).astype(F32) + 0.5) / group_width)
    col_group = jnp.floor((iota((channels, channels), 1).astype(F32) + 0.5) / group_width)
    same_group = jnp.where(row_group == col_group, 1.0, 0.0).astype(BF16)
    count = float(tokens * group_width)
    spot = jnp.bitwise_and(iota((tokens, channels), 0), W - 1)
    border = jnp.zeros((W, channels), BF16)
    for side in range(3):
        padded[side, 0:W] = border
        padded[side, W + tokens : W + tokens + W] = border

    def spread_act(act):
        padded[1, W : W + tokens] = act.astype(BF16)
        before = jnp.where(spot == 0, 0.0, pltpu.roll(act, 1, 0))
        padded[0, W : W + tokens] = before.astype(BF16)
        after = jnp.where(spot == W - 1, 0.0, pltpu.roll(act, tokens - 1, 0))
        padded[2, W : W + tokens] = after.astype(BF16)

    def convolve(weight, start, size):
        total = None
        for a in range(3):
            for b in range(3):
                term = dot(padded[b, start + W * a : start + W * a + size], weight[a, b])
                total = term if total is None else total + term
        return total

    local[3].wait()
    spread_act(gn_silu(x_ref[...].astype(F32), same_group, count))
    local[4].wait()
    inner = convolve(conv_a, 0, tokens)
    chain_step(0, 1)
    bias = time_parts[0, 0:1]
    for d in range(1, frames):
        time_copy(d).wait_recv()
        bias = bias + time_parts[d, 0:1]
    spread_act(gn_silu(inner + bias, same_group, count))
    local[5].wait()
    local[6].wait()
    local[7].wait()
    half = tokens // 2

    def near_copy(c):
        block = normed.at[video, c]
        return remote(block, block, near_send.at[c], near_recv.at[c], video=partner)

    def far_copy(d, c):
        block = normed.at[video, c]
        return remote(
            block, block, far_send.at[d - 1, c], far_recv.at[d - 1, c], video=video_at(d, core)
        )

    def relay_copy(d, c):
        block = normed.at[video_at(columns - d, core), c]
        return remote(
            block, block, relay_send.at[d - 1, c], relay_recv.at[d - 1, c], video=partner
        )

    for c in range(2):
        part = slice(c * half, (c + 1) * half)
        hidden = (x_ref[part].astype(F32) + convolve(conv_b, c * half, half)).astype(BF16)
        hidden_ref[part] = hidden
        normed[video, c] = layer_norm(hidden.astype(F32)).astype(BF16)
        for d in range(1, columns):
            far_copy(d, c).start()
        near_copy(c).start()
        if c == 0:
            chain_step(0, 2)
    for k in range(3, frames):
        chain_step(0, k)
    chain_step(1, 0)
    chain_finish(0)

    w_query, w_key, w_value = matrix(0, 0), matrix(0, 1), matrix(0, 2)

    def project(u):
        both = normed[u].reshape(tokens, channels)
        keys_ref[u] = dot(both, w_key).astype(BF16)
        values_ref[u] = dot(both, w_value).astype(BF16)

    queries = dot(normed[video].reshape(tokens, channels), w_query).astype(BF16)
    project(video)
    for d in range(1, columns):
        for c in range(2):
            block = normed.at[video_at(columns - d, core), c]
            remote(
                block, block, far_send.at[d - 1, c], far_recv.at[d - 1, c], video=video
            ).wait_recv()
            relay_copy(d, c).start()
        if d == 1:
            for c in range(2):
                block = normed.at[partner, c]
                remote(block, block, near_send.at[c], near_recv.at[c], video=partner).wait_recv()
            project(partner)
        project(video_at(columns - d, core))
    chain_step(1, 1)
    for d in range(1, columns):
        for c in range(2):
            block = normed.at[video_at(columns - d, 1 - core), c]
            remote(
                block, block, relay_send.at[d - 1, c], relay_recv.at[d - 1, c], video=partner
            ).wait_recv()
        project(video_at(columns - d, 1 - core))

    exponent = math.log2(math.e) / math.sqrt(head_width)
    w_out = matrix(0, 3)
    lane_row = iota((1, tokens), 1)
    ones = jnp.ones((tokens, 128), BF16)
    rows_per = tokens // chunks // frames

    def go_copy(c, d):
        to = lax.rem(frame + d, frames)
        return remote(
            send_blocks.at[c, to],
            recv_blocks.at[c, frame],
            go_send.at[c, d - 1],
            go_recv.at[c, d - 1],
            frame=to,
        )

    def ret_copy(c, d):
        to = lax.rem(frame + d, frames)
        return remote(
            back_blocks.at[c, to],
            final_blocks.at[c, frame],
            ret_send.at[c, d - 1],
            ret_recv.at[c, d - 1],
            frame=to,
        )

    def attend(i):
        part = slice(i * half, (i + 1) * half)
        blocks = [jnp.zeros((half, min(128, channels - s)), F32) for s in range(0, channels, 128)]
        for m in range(2):
            target = match_ref[m, video]
            keys = keys_ref[target]
            values = values_ref[target]
            bias_low = jnp.where(mask_ref[m, video, i, 0] > 0, 0.0, FILL)
            bias_high = jnp.where(mask_ref[m, video, i, 1] > 0, 0.0, FILL)
            bias_row = jnp.where(lane_row < half, bias_low, bias_high)
            for h in range(HEADS):
                low = h * head_width // 128 * 128
                high = min(-(-(h + 1) * head_width // 128) * 128, channels)
                lanes = iota((1, high - low), 1) + low
                inside = jnp.logical_and(lanes >= h * head_width, lanes < (h + 1) * head_width)
                inside = jnp.where(inside, 1.0, 0.0).astype(BF16)
                scores = dot_nt(queries[part, low:high] * inside, keys[:, low:high]) + bias_row
                peak = jnp.max(scores, axis=-1, keepdims=True)
                powers = jnp.exp2((scores - peak) * exponent).astype(BF16)
                total = 1.0 / dot(powers, ones)
                result = dot(powers, values[:, low:high] * inside)
                for s in range(low, high, 128):
                    width = min(128, channels - s)
                    blocks[s // 128] = (
                        blocks[s // 128]
                        + result[:, s - low : s - low + width] * total[:, :width]
                    )
        mixture = jnp.concatenate(blocks, axis=1).astype(BF16)
        second = (hidden_ref[part].astype(F32) + dot(mixture, w_out)).astype(BF16)
        second_ref[part] = second
        return layer_norm(second.astype(F32)).astype(BF16)

    def send_out(c, temp_normed):
        send_blocks[c] = temp_normed.reshape(frames, rows_per, channels)
        for d in range(1, frames):
            go_copy(c, d).start()
        recv_blocks[c, frame] = send_blocks[c, frame]

    if chunks == 2:
        send_out(0, attend(0))
        chain_step(1, 2)
        send_out(1, attend(1))
    else:
        first = attend(0)
        chain_step(1, 2)
        second_part = attend(1)
        send_out(0, jnp.concatenate([first, second_part], axis=0))
    for k in range(3, frames):
        chain_step(1, k)
    chain_finish(1)

    w_tq, w_tk, w_tv = matrix(1, 0), matrix(1, 1), matrix(1, 2)
    w_tout = matrix(1, 3)
    lane_head = jnp.floor((iota((channels, 128), 0).astype(F32) + 0.5) / head_width)
    gather_heads = jnp.where(
        lane_head == iota((channels, 128), 1).astype(F32), 1.0, 0.0
    ).astype(BF16)
    row_head = jnp.floor((iota((128, channels), 1).astype(F32) + 0.5) / head_width)
    spread_heads = jnp.where(
        row_head == iota((128, channels), 0).astype(F32), 1.0, 0.0
    ).astype(BF16)

    for c in range(chunks):
        for d in range(1, frames):
            block = recv_blocks.at[c, lax.rem(frame + frames - d, frames)]
            remote(
                block, block, go_send.at[c, d - 1], go_recv.at[c, d - 1], frame=frame
            ).wait_recv()
        stacked = recv_blocks[c].reshape(frames * rows_per, channels)
        q = dot(stacked, w_tq).astype(BF16).astype(F32)
        k = dot(stacked, w_tk).astype(BF16).astype(F32)
        v = dot(stacked, w_tv).astype(BF16).astype(F32)
        for f in range(frames):
            q_f = q[f * rows_per : (f + 1) * rows_per]
            product = jnp.concatenate([q_f] * frames, axis=0) * k
            coarse = product.astype(BF16)
            fine = (product - coarse.astype(F32)).astype(BF16)
            scores = dot(coarse, gather_heads) + dot(fine, gather_heads)
            parts = [scores[g * rows_per : (g + 1) * rows_per] for g in range(frames)]
            peak = functools.reduce(jnp.maximum, parts)
            parts = [jnp.exp2((p - peak) * exponent) for p in parts]
            scale = 1.0 / functools.reduce(jnp.add, parts)
            probs = jnp.concatenate([p * scale for p in parts], axis=0).astype(BF16)
            weighted = dot(probs, spread_heads) * v
            summed = functools.reduce(
                jnp.add, [weighted[g * rows_per : (g + 1) * rows_per] for g in range(frames)]
            )
            back_blocks[c, f] = summed.astype(BF16)
        for d in range(1, frames):
            ret_copy(c, d).start()
        final_blocks[c, frame] = back_blocks[c, frame]

    span = tokens // chunks
    for c in range(chunks):
        for d in range(1, frames):
            block = final_blocks.at[c, lax.rem(frame + frames - d, frames)]
            remote(
                block, block, ret_send.at[c, d - 1], ret_recv.at[c, d - 1], frame=frame
            ).wait_recv()
        part = slice(c * span, (c + 1) * span)
        outcome = final_blocks[c].reshape(span, channels)
        out_ref[0, 0, part] = (second_ref[part].astype(F32) + dot(outcome, w_tout)).astype(BF16)

    for d in range(1, frames):
        time_copy(d).wait_send()
        for c in range(chunks):
            go_copy(c, d).wait_send()
            ret_copy(c, d).wait_send()
    for c in range(2):
        near_copy(c).wait_send()
        for d in range(1, columns):
            far_copy(d, c).wait_send()
            relay_copy(d, c).wait_send()
    chain_drain(0)
    chain_drain(1)


def per_device(frames, videos, *args):
    (
        latents,
        timesteps,
        matchings,
        tile_mask,
        conv_first,
        conv_second,
        time_proj,
        epi_in,
        epi_out,
        temp_in,
        temp_out,
    ) = args
    tokens, channels = latents.shape[2:]
    rows = epi_out.shape[0]
    columns = videos // 2
    chunks = 2 if (tokens // 2 // frames) % 16 == 0 else 1
    block = (chunks, frames, tokens // chunks // frames, channels)
    dma = pltpu.SemaphoreType.DMA
    hops = max(columns - 1, 1)
    anywhere = pl.BlockSpec(memory_space=pl.ANY)
    scalar = pl.BlockSpec(memory_space=pltpu.SMEM)
    return pl.pallas_call(
        functools.partial(kernel, frames, videos, chunks),
        out_shape=jax.ShapeDtypeStruct(latents.shape, BF16),
        in_specs=[scalar] * 3 + [anywhere] * 8,
        out_specs=pl.BlockSpec(memory_space=pltpu.VMEM),
        scratch_shapes=[
            pltpu.VMEM((tokens, channels), BF16),
            pltpu.VMEM(conv_first.shape, BF16),
            pltpu.VMEM(conv_second.shape, BF16),
            pltpu.VMEM(time_proj.shape, BF16),
            pltpu.VMEM((frames, 8, channels), F32),
            pltpu.VMEM((2, frames, 4, rows, channels), BF16),
            pltpu.VMEM((3, tokens + 2 * W, channels), BF16),
            pltpu.VMEM((tokens, channels), BF16),
            pltpu.VMEM((videos, 2, tokens // 2, channels), BF16),
            pltpu.VMEM((videos, tokens, channels), BF16),
            pltpu.VMEM((videos, tokens, channels), BF16),
            pltpu.VMEM((tokens, channels), BF16),
            pltpu.VMEM(block, BF16),
            pltpu.VMEM(block, BF16),
            pltpu.VMEM(block, BF16),
            pltpu.VMEM(block, BF16),
            dma((8,)),
            dma((frames,)),
            dma((frames,)),
            dma((2, 2, frames)),
            dma((2, 2, frames)),
            dma((2, 2, frames)),
            dma((2, 2, frames)),
            dma((2,)),
            dma((2,)),
            dma((hops, 2)),
            dma((hops, 2)),
            dma((hops, 2)),
            dma((hops, 2)),
            dma((chunks, frames)),
            dma((chunks, frames)),
            dma((chunks, frames)),
            dma((chunks, frames)),
        ],
        compiler_params=pltpu.CompilerParams(collective_id=0, has_side_effects=True),
    )(
        timesteps,
        matchings,
        tile_mask,
        latents,
        conv_first,
        conv_second,
        time_proj,
        epi_in,
        epi_out,
        temp_in,
        temp_out,
    )


def solution(mesh):
    placed = (
        P(("groups", "video"), "frame", None, None),
        P(("groups", "video")),
        P(None, "groups"),
        P(None, "groups", None, None),
        P(),
        P(),
        P("frame", None),
        P(None, "frame", None),
        P("frame", None),
        P(None, "frame", None),
        P("frame", None),
    )
    return jax.shard_map(
        functools.partial(per_device, mesh.shape["frame"], mesh.shape["video"]),
        mesh=mesh,
        in_specs=placed,
        out_specs=P(("groups", "video"), "frame", None, None),
        check_vma=False,
    )
```

```python
import functools
import math

import jax
import jax.numpy as jnp
from jax import lax
from jax.experimental import pallas as pl
from jax.experimental.pallas import tpu as pltpu
from jax.sharding import PartitionSpec as P

HEADS = 8
NORM_GROUPS = 32
TEMB = 1280
H = 8
W = 32
EPS = 1e-05
FILL = -1e30
F32 = jnp.float32
BF16 = jnp.bfloat16
MESH = pl.DeviceIdType.MESH


def dot(a, b):
    return jnp.dot(a, b, preferred_element_type=F32)


def dot_nt(a, b):
    return lax.dot_general(a, b, (((1,), (1,)), ((), ())), preferred_element_type=F32)


def iota(shape, dim):
    return lax.broadcasted_iota(jnp.int32, shape, dim)


def split_rows(row):
    hi = row.astype(BF16).astype(F32)
    rest = row - hi
    mid = rest.astype(BF16).astype(F32)
    low = rest - mid
    which = iota((16, row.shape[1]), 0)
    packed = jnp.where(which == 0, hi, jnp.where(which == 1, mid, jnp.where(which == 2, low, 0.0)))
    return packed.astype(BF16)


def group_total(row, same_group):
    return jnp.sum(dot(split_rows(row), same_group), axis=0, keepdims=True)


def gn_silu(values, same_group, count):
    average = group_total(jnp.sum(values, axis=0, keepdims=True), same_group) * (1.0 / count)
    centered = values - average
    spread = group_total(jnp.sum(centered * centered, axis=0, keepdims=True), same_group) * (
        1.0 / count
    )
    u = centered * (1.0 / jnp.sqrt(spread + EPS))
    return u * (1.0 / (1.0 + jnp.exp(-u)))


def layer_norm(values):
    average = jnp.mean(values, axis=-1, keepdims=True)
    centered = values - average
    spread = jnp.mean(centered * centered, axis=-1, keepdims=True)
    return centered * (1.0 / jnp.sqrt(spread + EPS))


def wave(angle, quarter_shift):
    n = jnp.floor(angle * (2.0 / math.pi) + 0.5)
    r = ((angle - n * 1.5703125) - n * 4.837512969970703125e-4) - n * 7.54978995489188216e-8
    z = r * r
    sin_r = r + r * z * (
        -1.6666654611e-1 + z * (8.3321608736e-3 + z * -1.9515295891e-4)
    )
    cos_r = (
        1.0
        - 0.5 * z
        + z * z * (4.166664568298827e-2 + z * (-1.388731625493765e-3 + z * 2.443315711809948e-5))
    )
    q = n + quarter_shift
    q = q - 4.0 * jnp.floor(q * 0.25)
    return jnp.where(
        q < 0.5, cos_r, jnp.where(q < 1.5, -sin_r, jnp.where(q < 2.5, -cos_r, sin_r))
    )


def kernel(
    frames,
    videos,
    chunks,
    steps_ref,
    match_ref,
    mask_ref,
    x_hbm,
    conv_a_hbm,
    conv_b_hbm,
    time_hbm,
    epi_in_hbm,
    epi_out_hbm,
    temp_in_hbm,
    temp_out_hbm,
    out_ref,
    xt_ref,
    x_ref,
    conv_a,
    conv_b,
    time_w,
    time_parts,
    weights,
    padded,
    hidden_ref,
    normed,
    keys_ref,
    values_ref,
    second_ref,
    send_blocks,
    recv_blocks,
    back_blocks,
    final_blocks,
    local_sem,
    time_send,
    time_recv,
    chain_send,
    chain_recv,
    pair_send,
    pair_recv,
    near_send,
    near_recv,
    far_send,
    far_recv,
    relay_send,
    relay_recv,
    go_send,
    go_recv,
    ret_send,
    ret_recv,
):
    channels, tokens = xt_ref.shape
    head_width = channels // HEADS
    frame = lax.axis_index("frame")
    video = lax.axis_index("video")
    core = lax.rem(video, 2)
    column = video // 2
    columns = videos // 2
    partner = column * 2 + (1 - core)
    last = frames - 1

    def video_at(shift, which):
        return lax.rem(column + shift, columns) * 2 + which

    barrier = pltpu.get_barrier_semaphore()
    for d in range(1, frames):
        pl.semaphore_signal(
            barrier, inc=1, device_id={"frame": lax.rem(frame + d, frames)}, device_id_type=MESH
        )
    pl.semaphore_signal(barrier, inc=1, device_id={"video": partner}, device_id_type=MESH)
    for d in range(1, columns):
        pl.semaphore_signal(
            barrier, inc=1, device_id={"video": video_at(d, core)}, device_id_type=MESH
        )

    local = [
        (time_hbm, time_w),
        (epi_in_hbm.at[1], weights.at[frame, 0]),
        (epi_in_hbm.at[2], weights.at[frame, 1]),
        (x_hbm.at[0, 0], xt_ref),
        (epi_in_hbm.at[0], weights.at[frame, 2]),
        (epi_out_hbm, weights.at[frame, 3]),
        (conv_a_hbm, conv_a),
        (conv_b_hbm, conv_b),
        (temp_in_hbm.at[1], weights.at[frame, 4]),
        (temp_in_hbm.at[2], weights.at[frame, 5]),
        (temp_in_hbm.at[0], weights.at[frame, 6]),
        (temp_out_hbm, weights.at[frame, 7]),
    ]
    local = [pltpu.make_async_copy(a, b, local_sem.at[i]) for i, (a, b) in enumerate(local)]
    for copy in local:
        copy.start()
    pl.semaphore_wait(barrier, frames + columns - 1)

    def remote(src, dst, send, recv, **where):
        return pltpu.make_async_remote_copy(
            src_ref=src,
            dst_ref=dst,
            send_sem=send,
            recv_sem=recv,
            device_id=where,
            device_id_type=MESH,
        )


    def owner(direction, k):
        return frame - k if direction == 0 else frame + k

    def has(direction, k):
        return frame >= k if direction == 0 else frame + k <= last

    def can_pass(direction):
        return frame < last if direction == 0 else frame > 0

    def chain_copy(s, direction, k):
        block = weights.at[owner(direction, k), s * 2 + core]
        to = frame + 1 if direction == 0 else frame - 1
        return remote(
            block, block, chain_send.at[s, direction, k], chain_recv.at[s, direction, k], frame=to
        )

    def pair_copy(s, direction, k):
        block = weights.at[owner(direction, k), s * 2 + core]
        return remote(
            block, block, pair_send.at[s, direction, k], pair_recv.at[s, direction, k], video=partner
        )

    def chain_step(s, k):
        for direction in range(2):
            if k > 0:

                @pl.when(has(direction, k))
                def _():
                    chain_copy_recv(s, direction, k - 1)
                    pair_copy(s, direction, k).start()

            if k < last:

                @pl.when(jnp.logical_and(has(direction, k), can_pass(direction)))
                def _():
                    chain_copy(s, direction, k).start()

    def chain_copy_recv(s, direction, k):
        block = weights.at[owner(direction, k + 1), s * 2 + core]
        remote(
            block, block, chain_send.at[s, direction, k], chain_recv.at[s, direction, k], frame=frame
        ).wait_recv()

    def chain_finish(s):
        for direction in range(2):
            for k in range(1, frames):

                @pl.when(has(direction, k))
                def _():
                    block = weights.at[owner(direction, k), s * 2 + 1 - core]
                    remote(
                        block,
                        block,
                        pair_send.at[s, direction, k],
                        pair_recv.at[s, direction, k],
                        video=partner,
                    ).wait_recv()

    def chain_drain(s):
        for direction in range(2):
            for k in range(frames):
                if k > 0:

                    @pl.when(has(direction, k))
                    def _():
                        pair_copy(s, direction, k).wait_send()

                if k < last:

                    @pl.when(jnp.logical_and(has(direction, k), can_pass(direction)))
                    def _():
                        chain_copy(s, direction, k).wait_send()

    def matrix(index):
        return jnp.concatenate([weights[f, index] for f in range(frames)], axis=0)

    local[0].wait()
    rows = time_w.shape[0]
    place = iota((16, rows), 1) + frame * rows
    is_sin = place >= TEMB // 2
    index = jnp.where(is_sin, place - TEMB // 2, place).astype(F32)
    frequency = jnp.exp(-math.log(10000.0) * index / (TEMB // 2))
    angle = frequency * steps_ref[0].astype(F32)
    basis = wave(angle, jnp.where(is_sin, 3.0, 0.0))
    time_act = (basis * (1.0 / (1.0 + jnp.exp(-basis)))).astype(BF16)
    time_parts[0] = dot(time_act, time_w[...])[0:8]

    def time_copy(d):
        return remote(
            time_parts.at[0],
            time_parts.at[d],
            time_send.at[d - 1],
            time_recv.at[d - 1],
            frame=lax.rem(frame + d, frames),
        )

    for d in range(1, frames):
        time_copy(d).start()
    local[1].wait()
    local[2].wait()
    chain_step(0, 0)
    local[4].wait()
    local[5].wait()
    chain_step(1, 0)

    group_width = channels // NORM_GROUPS
    row_group = jnp.floor((iota((channels, channels), 0).astype(F32) + 0.5) / group_width)
    col_group = jnp.floor((iota((channels, channels), 1).astype(F32) + 0.5) / group_width)
    same_group = jnp.where(row_group == col_group, 1.0, 0.0).astype(BF16)
    count = float(tokens * group_width)
    spot = jnp.bitwise_and(iota((tokens, channels), 0), W - 1)
    border = jnp.zeros((W, channels), BF16)
    for side in range(3):
        padded[side, 0:W] = border
        padded[side, W + tokens : W + tokens + W] = border

    def spread_act(act):
        padded[1, W : W + tokens] = act.astype(BF16)
        before = jnp.where(spot == 0, 0.0, pltpu.roll(act, 1, 0))
        padded[0, W : W + tokens] = before.astype(BF16)
        after = jnp.where(spot == W - 1, 0.0, pltpu.roll(act, tokens - 1, 0))
        padded[2, W : W + tokens] = after.astype(BF16)

    def convolve(weight, start, size):
        total = None
        for a in range(3):
            for b in range(3):
                term = dot(padded[b, start + W * a : start + W * a + size], weight[a, b])
                total = term if total is None else total + term
        return total

    local[3].wait()
    source = jnp.transpose(xt_ref[...].astype(F32))
    x_ref[...] = source.astype(BF16)
    spread_act(gn_silu(source, same_group, count))
    local[6].wait()
    inner = convolve(conv_a, 0, tokens)
    chain_step(0, 1)
    bias = time_parts[0, 0:1]
    for d in range(1, frames):
        time_copy(d).wait_recv()
        bias = bias + time_parts[d, 0:1]
    spread_act(gn_silu(inner + bias, same_group, count))
    chain_step(1, 1)
    local[7].wait()
    half = tokens // 2

    def near_copy(c):
        block = normed.at[video, c]
        return remote(block, block, near_send.at[c], near_recv.at[c], video=partner)

    def far_copy(d, c):
        block = normed.at[video, c]
        return remote(
            block, block, far_send.at[d - 1, c], far_recv.at[d - 1, c], video=video_at(d, core)
        )

    def relay_copy(d, c):
        block = normed.at[video_at(columns - d, core), c]
        return remote(
            block, block, relay_send.at[d - 1, c], relay_recv.at[d - 1, c], video=partner
        )

    for c in range(2):
        part = slice(c * half, (c + 1) * half)
        hidden = (x_ref[part].astype(F32) + convolve(conv_b, c * half, half)).astype(BF16)
        hidden_ref[part] = hidden
        normed[video, c] = layer_norm(hidden.astype(F32)).astype(BF16)
        for d in range(1, columns):
            far_copy(d, c).start()
        near_copy(c).start()
        chain_step(c, 2)
    for copy in local[8:]:
        copy.wait()
    for s in range(2):
        for k in range(3, frames):
            chain_step(s, k)
        chain_step(s + 2, 0)
    chain_finish(0)

    w_key, w_value = matrix(0), matrix(1)

    def project(u):
        both = normed[u].reshape(tokens, channels)
        keys_ref[u] = dot(both, w_key).astype(BF16)
        values_ref[u] = dot(both, w_value).astype(BF16)

    project(video)
    for d in range(1, columns):
        for c in range(2):
            block = normed.at[video_at(columns - d, core), c]
            remote(
                block, block, far_send.at[d - 1, c], far_recv.at[d - 1, c], video=video
            ).wait_recv()
            relay_copy(d, c).start()
        if d == 1:
            for c in range(2):
                block = normed.at[partner, c]
                remote(block, block, near_send.at[c], near_recv.at[c], video=partner).wait_recv()
            project(partner)
        project(video_at(columns - d, core))
    chain_step(2, 1)
    chain_finish(1)
    queries = dot(normed[video].reshape(tokens, channels), matrix(2)).astype(BF16)
    chain_step(3, 1)
    for d in range(1, columns):
        for c in range(2):
            block = normed.at[video_at(columns - d, 1 - core), c]
            remote(
                block, block, relay_send.at[d - 1, c], relay_recv.at[d - 1, c], video=partner
            ).wait_recv()
        project(video_at(columns - d, 1 - core))

    exponent = math.log2(math.e) / math.sqrt(head_width)
    w_out = matrix(3)
    lane_row = iota((1, tokens), 1)
    ones = jnp.ones((tokens, 128), BF16)
    rows_per = tokens // chunks // frames

    def go_copy(c, d):
        to = lax.rem(frame + d, frames)
        return remote(
            send_blocks.at[c, to],
            recv_blocks.at[c, frame],
            go_send.at[c, d - 1],
            go_recv.at[c, d - 1],
            frame=to,
        )

    def ret_copy(c, d):
        to = lax.rem(frame + d, frames)
        return remote(
            back_blocks.at[c, to],
            final_blocks.at[c, frame],
            ret_send.at[c, d - 1],
            ret_recv.at[c, d - 1],
            frame=to,
        )

    def attend(i):
        part = slice(i * half, (i + 1) * half)
        blocks = [jnp.zeros((half, min(128, channels - s)), F32) for s in range(0, channels, 128)]
        for m in range(2):
            target = match_ref[m, video]
            keys = keys_ref[target]
            values = values_ref[target]
            bias_low = jnp.where(mask_ref[m, i, 0, video] > 0, 0.0, FILL)
            bias_high = jnp.where(mask_ref[m, i, 1, video] > 0, 0.0, FILL)
            bias_row = jnp.where(lane_row < half, bias_low, bias_high)
            for h in range(HEADS):
                low = h * head_width // 128 * 128
                high = min(-(-(h + 1) * head_width // 128) * 128, channels)
                lanes = iota((1, high - low), 1) + low
                inside = jnp.logical_and(lanes >= h * head_width, lanes < (h + 1) * head_width)
                inside = jnp.where(inside, 1.0, 0.0).astype(BF16)
                scores = dot_nt(queries[part, low:high] * inside, keys[:, low:high]) + bias_row
                peak = jnp.max(scores, axis=-1, keepdims=True)
                powers = jnp.exp2((scores - peak) * exponent).astype(BF16)
                total = 1.0 / dot(powers, ones)
                result = dot(powers, values[:, low:high] * inside)
                for s in range(low, high, 128):
                    width = min(128, channels - s)
                    blocks[s // 128] = (
                        blocks[s // 128]
                        + result[:, s - low : s - low + width] * total[:, :width]
                    )
        mixture = jnp.concatenate(blocks, axis=1).astype(BF16)
        second = (hidden_ref[part].astype(F32) + dot(mixture, w_out)).astype(BF16)
        second_ref[part] = second
        return layer_norm(second.astype(F32)).astype(BF16)

    def send_out(c, temp_normed):
        send_blocks[c] = temp_normed.reshape(frames, rows_per, channels)
        for d in range(1, frames):
            go_copy(c, d).start()
        recv_blocks[c, frame] = send_blocks[c, frame]

    if chunks == 2:
        send_out(0, attend(0))
        chain_step(2, 2)
        chain_step(3, 2)
        send_out(1, attend(1))
    else:
        first = attend(0)
        chain_step(2, 2)
        chain_step(3, 2)
        second_part = attend(1)
        send_out(0, jnp.concatenate([first, second_part], axis=0))
    for s in range(2, 4):
        for k in range(3, frames):
            chain_step(s, k)
    chain_finish(2)
    chain_finish(3)

    w_tk, w_tv, w_tq, w_tout = matrix(4), matrix(5), matrix(6), matrix(7)
    lane_head = jnp.floor((iota((channels, 128), 0).astype(F32) + 0.5) / head_width)
    gather_heads = jnp.where(
        lane_head == iota((channels, 128), 1).astype(F32), 1.0, 0.0
    ).astype(BF16)
    row_head = jnp.floor((iota((128, channels), 1).astype(F32) + 0.5) / head_width)
    spread_heads = jnp.where(
        row_head == iota((128, channels), 0).astype(F32), 1.0, 0.0
    ).astype(BF16)

    for c in range(chunks):
        for d in range(1, frames):
            block = recv_blocks.at[c, lax.rem(frame + frames - d, frames)]
            remote(
                block, block, go_send.at[c, d - 1], go_recv.at[c, d - 1], frame=frame
            ).wait_recv()
        stacked = recv_blocks[c].reshape(frames * rows_per, channels)
        q = dot(stacked, w_tq).astype(BF16).astype(F32)
        k = dot(stacked, w_tk).astype(BF16).astype(F32)
        v = dot(stacked, w_tv).astype(BF16).astype(F32)
        for f in range(frames):
            q_f = q[f * rows_per : (f + 1) * rows_per]
            product = jnp.concatenate([q_f] * frames, axis=0) * k
            coarse = product.astype(BF16)
            fine = (product - coarse.astype(F32)).astype(BF16)
            scores = dot(coarse, gather_heads) + dot(fine, gather_heads)
            parts = [scores[g * rows_per : (g + 1) * rows_per] for g in range(frames)]
            peak = functools.reduce(jnp.maximum, parts)
            parts = [jnp.exp2((p - peak) * exponent) for p in parts]
            scale = 1.0 / functools.reduce(jnp.add, parts)
            probs = jnp.concatenate([p * scale for p in parts], axis=0).astype(BF16)
            weighted = dot(probs, spread_heads) * v
            summed = functools.reduce(
                jnp.add, [weighted[g * rows_per : (g + 1) * rows_per] for g in range(frames)]
            )
            back_blocks[c, f] = summed.astype(BF16)
        for d in range(1, frames):
            ret_copy(c, d).start()
        final_blocks[c, frame] = back_blocks[c, frame]

    span = tokens // chunks
    for c in range(chunks):
        for d in range(1, frames):
            block = final_blocks.at[c, lax.rem(frame + frames - d, frames)]
            remote(
                block, block, ret_send.at[c, d - 1], ret_recv.at[c, d - 1], frame=frame
            ).wait_recv()
        part = slice(c * span, (c + 1) * span)
        outcome = final_blocks[c].reshape(span, channels)
        result = second_ref[part].astype(F32) + dot(outcome, w_tout)
        out_ref[0, 0, :, part] = jnp.transpose(result).astype(BF16)

    for d in range(1, frames):
        time_copy(d).wait_send()
        for c in range(chunks):
            go_copy(c, d).wait_send()
            ret_copy(c, d).wait_send()
    for c in range(2):
        near_copy(c).wait_send()
        for d in range(1, columns):
            far_copy(d, c).wait_send()
            relay_copy(d, c).wait_send()
    for s in range(4):
        chain_drain(s)


def per_device(frames, videos, *args):
    (
        latents,
        timesteps,
        matchings,
        tile_mask,
        conv_first,
        conv_second,
        time_proj,
        epi_in,
        epi_out,
        temp_in,
        temp_out,
    ) = args
    tokens, channels = latents.shape[2:]
    rows = epi_out.shape[0]
    columns = videos // 2
    chunks = 2 if (tokens // 2 // frames) % 16 == 0 else 1
    block = (chunks, frames, tokens // chunks // frames, channels)
    dma = pltpu.SemaphoreType.DMA
    hops = max(columns - 1, 1)
    anywhere = pl.BlockSpec(memory_space=pl.ANY)
    scalar = pl.BlockSpec(memory_space=pltpu.SMEM)
    result = pl.pallas_call(
        functools.partial(kernel, frames, videos, chunks),
        out_shape=jax.ShapeDtypeStruct((1, 1, channels, tokens), BF16),
        in_specs=[scalar] * 3 + [anywhere] * 8,
        out_specs=pl.BlockSpec(memory_space=pltpu.VMEM),
        scratch_shapes=[
            pltpu.VMEM((channels, tokens), BF16),
            pltpu.VMEM((tokens, channels), BF16),
            pltpu.VMEM(conv_first.shape, BF16),
            pltpu.VMEM(conv_second.shape, BF16),
            pltpu.VMEM(time_proj.shape, BF16),
            pltpu.VMEM((frames, 8, channels), F32),
            pltpu.VMEM((frames, 8, rows, channels), BF16),
            pltpu.VMEM((3, tokens + 2 * W, channels), BF16),
            pltpu.VMEM((tokens, channels), BF16),
            pltpu.VMEM((videos, 2, tokens // 2, channels), BF16),
            pltpu.VMEM((videos, tokens, channels), BF16),
            pltpu.VMEM((videos, tokens, channels), BF16),
            pltpu.VMEM((tokens, channels), BF16),
            pltpu.VMEM(block, BF16),
            pltpu.VMEM(block, BF16),
            pltpu.VMEM(block, BF16),
            pltpu.VMEM(block, BF16),
            dma((12,)),
            dma((frames,)),
            dma((frames,)),
            dma((4, 2, frames)),
            dma((4, 2, frames)),
            dma((4, 2, frames)),
            dma((4, 2, frames)),
            dma((2,)),
            dma((2,)),
            dma((hops, 2)),
            dma((hops, 2)),
            dma((hops, 2)),
            dma((hops, 2)),
            dma((chunks, frames)),
            dma((chunks, frames)),
            dma((chunks, frames)),
            dma((chunks, frames)),
        ],
        compiler_params=pltpu.CompilerParams(collective_id=0, has_side_effects=True),
    )(
        timesteps,
        matchings,
        jnp.transpose(tile_mask, (0, 2, 3, 1)),
        jnp.swapaxes(latents, 2, 3),
        conv_first,
        conv_second,
        time_proj,
        epi_in,
        epi_out,
        temp_in,
        temp_out,
    )
    return jnp.swapaxes(result, 2, 3)


def solution(mesh):
    placed = (
        P(("groups", "video"), "frame", None, None),
        P(("groups", "video")),
        P(None, "groups"),
        P(None, "groups", None, None),
        P(),
        P(),
        P("frame", None),
        P(None, "frame", None),
        P("frame", None),
        P(None, "frame", None),
        P("frame", None),
    )
    return jax.shard_map(
        functools.partial(per_device, mesh.shape["frame"], mesh.shape["video"]),
        mesh=mesh,
        in_specs=placed,
        out_specs=P(("groups", "video"), "frame", None, None),
        check_vma=False,
    )
```

```python
import functools
import math

import jax
import jax.numpy as jnp
from jax import lax
from jax.experimental import pallas as pl
from jax.experimental.pallas import tpu as pltpu
from jax.sharding import PartitionSpec as P

HEADS = 8
NORM_GROUPS = 32
TEMB = 1280
H = 8
W = 32
EPS = 1e-05
FILL = -1e30
F32 = jnp.float32
BF16 = jnp.bfloat16
MESH = pl.DeviceIdType.MESH


def dot(a, b):
    return jnp.dot(a, b, preferred_element_type=F32)


def dot_nt(a, b):
    return lax.dot_general(a, b, (((1,), (1,)), ((), ())), preferred_element_type=F32)


def iota(shape, dim):
    return lax.broadcasted_iota(jnp.int32, shape, dim)


def split_rows(row):
    hi = row.astype(BF16).astype(F32)
    rest = row - hi
    mid = rest.astype(BF16).astype(F32)
    low = rest - mid
    which = iota((16, row.shape[1]), 0)
    packed = jnp.where(which == 0, hi, jnp.where(which == 1, mid, jnp.where(which == 2, low, 0.0)))
    return packed.astype(BF16)


def group_total(row, same_group):
    return jnp.sum(dot(split_rows(row), same_group), axis=0, keepdims=True)


def gn_silu(values, same_group, count):
    average = group_total(jnp.sum(values, axis=0, keepdims=True), same_group) * (1.0 / count)
    centered = values - average
    spread = group_total(jnp.sum(centered * centered, axis=0, keepdims=True), same_group) * (
        1.0 / count
    )
    u = centered * (1.0 / jnp.sqrt(spread + EPS))
    return u * (1.0 / (1.0 + jnp.exp(-u)))


def layer_norm(values):
    average = jnp.mean(values, axis=-1, keepdims=True)
    centered = values - average
    spread = jnp.mean(centered * centered, axis=-1, keepdims=True)
    return centered * (1.0 / jnp.sqrt(spread + EPS))


def wave(angle, quarter_shift):
    n = jnp.floor(angle * (2.0 / math.pi) + 0.5)
    r = ((angle - n * 1.5703125) - n * 4.837512969970703125e-4) - n * 7.54978995489188216e-8
    z = r * r
    sin_r = r + r * z * (
        -1.6666654611e-1 + z * (8.3321608736e-3 + z * -1.9515295891e-4)
    )
    cos_r = (
        1.0
        - 0.5 * z
        + z * z * (4.166664568298827e-2 + z * (-1.388731625493765e-3 + z * 2.443315711809948e-5))
    )
    q = n + quarter_shift
    q = q - 4.0 * jnp.floor(q * 0.25)
    return jnp.where(
        q < 0.5, cos_r, jnp.where(q < 1.5, -sin_r, jnp.where(q < 2.5, -cos_r, sin_r))
    )


def kernel(
    frames,
    videos,
    chunks,
    steps_hbm,
    match_hbm,
    mask_hbm,
    x_hbm,
    conv_a_hbm,
    conv_b_hbm,
    time_hbm,
    epi_in_hbm,
    epi_out_hbm,
    temp_in_hbm,
    temp_out_hbm,
    out_ref,
    steps_ref,
    match_ref,
    mask_ref,
    xt_ref,
    x_ref,
    conv_a,
    conv_b,
    time_w,
    time_parts,
    weights,
    padded,
    hidden_ref,
    normed,
    keys_ref,
    values_ref,
    second_ref,
    send_blocks,
    recv_blocks,
    back_blocks,
    final_blocks,
    local_sem,
    time_send,
    time_recv,
    chain_send,
    chain_recv,
    pair_send,
    pair_recv,
    near_send,
    near_recv,
    far_send,
    far_recv,
    relay_send,
    relay_recv,
    go_send,
    go_recv,
    ret_send,
    ret_recv,
):
    channels, tokens = xt_ref.shape
    head_width = channels // HEADS
    frame = lax.axis_index("frame")
    video = lax.axis_index("video")
    core = lax.rem(video, 2)
    column = video // 2
    columns = videos // 2
    partner = column * 2 + (1 - core)
    last = frames - 1

    def video_at(shift, which):
        return lax.rem(column + shift, columns) * 2 + which

    barrier = pltpu.get_barrier_semaphore()
    for d in range(1, frames):
        pl.semaphore_signal(
            barrier, inc=1, device_id={"frame": lax.rem(frame + d, frames)}, device_id_type=MESH
        )
    pl.semaphore_signal(barrier, inc=1, device_id={"video": partner}, device_id_type=MESH)
    for d in range(1, columns):
        pl.semaphore_signal(
            barrier, inc=1, device_id={"video": video_at(d, core)}, device_id_type=MESH
        )

    local = [
        (time_hbm, time_w),
        (epi_in_hbm.at[1], weights.at[frame, 0]),
        (epi_in_hbm.at[2], weights.at[frame, 1]),
        (x_hbm.at[0, 0], xt_ref),
        (epi_in_hbm.at[0], weights.at[frame, 2]),
        (epi_out_hbm, weights.at[frame, 3]),
        (conv_a_hbm, conv_a),
        (conv_b_hbm, conv_b),
        (temp_in_hbm.at[1], weights.at[frame, 4]),
        (temp_in_hbm.at[2], weights.at[frame, 5]),
        (temp_in_hbm.at[0], weights.at[frame, 6]),
        (temp_out_hbm, weights.at[frame, 7]),
        (steps_hbm, steps_ref),
        (match_hbm, match_ref),
        (mask_hbm, mask_ref),
    ]
    local = [pltpu.make_async_copy(a, b, local_sem.at[i]) for i, (a, b) in enumerate(local)]
    for i in (12, 0, 3, 1, 2, 4, 5, 6, 7, 8, 9, 10, 11, 13, 14):
        local[i].start()

    def remote(src, dst, send, recv, **where):
        return pltpu.make_async_remote_copy(
            src_ref=src,
            dst_ref=dst,
            send_sem=send,
            recv_sem=recv,
            device_id=where,
            device_id_type=MESH,
        )


    def owner(direction, k):
        return frame - k if direction == 0 else frame + k

    def has(direction, k):
        return frame >= k if direction == 0 else frame + k <= last

    def can_pass(direction):
        return frame < last if direction == 0 else frame > 0

    def chain_copy(s, direction, k):
        block = weights.at[owner(direction, k), s * 2 + core]
        to = frame + 1 if direction == 0 else frame - 1
        return remote(
            block, block, chain_send.at[s, direction, k], chain_recv.at[s, direction, k], frame=to
        )

    def pair_copy(s, direction, k):
        block = weights.at[owner(direction, k), s * 2 + core]
        return remote(
            block, block, pair_send.at[s, direction, k], pair_recv.at[s, direction, k], video=partner
        )

    def chain_step(s, k):
        for direction in range(2):
            if k > 0:

                @pl.when(has(direction, k))
                def _():
                    chain_copy_recv(s, direction, k - 1)
                    pair_copy(s, direction, k).start()

            if k < last:

                @pl.when(jnp.logical_and(has(direction, k), can_pass(direction)))
                def _():
                    chain_copy(s, direction, k).start()

    def chain_copy_recv(s, direction, k):
        block = weights.at[owner(direction, k + 1), s * 2 + core]
        remote(
            block, block, chain_send.at[s, direction, k], chain_recv.at[s, direction, k], frame=frame
        ).wait_recv()

    def chain_finish(s):
        for direction in range(2):
            for k in range(1, frames):

                @pl.when(has(direction, k))
                def _():
                    block = weights.at[owner(direction, k), s * 2 + 1 - core]
                    remote(
                        block,
                        block,
                        pair_send.at[s, direction, k],
                        pair_recv.at[s, direction, k],
                        video=partner,
                    ).wait_recv()

    def chain_drain(s):
        for direction in range(2):
            for k in range(frames):
                if k > 0:

                    @pl.when(has(direction, k))
                    def _():
                        pair_copy(s, direction, k).wait_send()

                if k < last:

                    @pl.when(jnp.logical_and(has(direction, k), can_pass(direction)))
                    def _():
                        chain_copy(s, direction, k).wait_send()

    def matrix(index):
        return jnp.concatenate([weights[f, index] for f in range(frames)], axis=0)

    local[12].wait()
    local[0].wait()
    rows = time_w.shape[0]
    place = iota((16, rows), 1) + frame * rows
    is_sin = place >= TEMB // 2
    index = jnp.where(is_sin, place - TEMB // 2, place).astype(F32)
    frequency = jnp.exp(-math.log(10000.0) * index / (TEMB // 2))
    angle = frequency * steps_ref[0].astype(F32)
    basis = wave(angle, jnp.where(is_sin, 3.0, 0.0))
    time_act = (basis * (1.0 / (1.0 + jnp.exp(-basis)))).astype(BF16)
    time_parts[0] = dot(time_act, time_w[...])[0:8]

    def time_copy(d):
        return remote(
            time_parts.at[0],
            time_parts.at[d],
            time_send.at[d - 1],
            time_recv.at[d - 1],
            frame=lax.rem(frame + d, frames),
        )


    group_width = channels // NORM_GROUPS
    row_group = jnp.floor((iota((channels, channels), 0).astype(F32) + 0.5) / group_width)
    col_group = jnp.floor((iota((channels, channels), 1).astype(F32) + 0.5) / group_width)
    same_group = jnp.where(row_group == col_group, 1.0, 0.0).astype(BF16)
    count = float(tokens * group_width)
    spot = jnp.bitwise_and(iota((tokens, channels), 0), W - 1)
    border = jnp.zeros((W, channels), BF16)
    for side in range(3):
        padded[side, 0:W] = border
        padded[side, W + tokens : W + tokens + W] = border

    def spread_act(act):
        padded[1, W : W + tokens] = act.astype(BF16)
        before = jnp.where(spot == 0, 0.0, pltpu.roll(act, 1, 0))
        padded[0, W : W + tokens] = before.astype(BF16)
        after = jnp.where(spot == W - 1, 0.0, pltpu.roll(act, tokens - 1, 0))
        padded[2, W : W + tokens] = after.astype(BF16)

    def convolve(weight, start, size):
        total = None
        for a in range(3):
            for b in range(3):
                term = dot(padded[b, start + W * a : start + W * a + size], weight[a, b])
                total = term if total is None else total + term
        return total

    local[3].wait()
    source = jnp.transpose(xt_ref[...].astype(F32))
    x_ref[...] = source.astype(BF16)
    spread_act(gn_silu(source, same_group, count))
    for i in (1, 2, 4, 5):
        local[i].wait()
    pl.semaphore_wait(barrier, frames + columns - 1)
    for d in range(1, frames):
        time_copy(d).start()
    chain_step(0, 0)
    chain_step(1, 0)
    local[6].wait()
    inner = convolve(conv_a, 0, tokens)
    chain_step(0, 1)
    bias = time_parts[0, 0:1]
    for d in range(1, frames):
        time_copy(d).wait_recv()
        bias = bias + time_parts[d, 0:1]
    spread_act(gn_silu(inner + bias, same_group, count))
    chain_step(1, 1)
    local[7].wait()
    half = tokens // 2

    def near_copy(c):
        block = normed.at[video, c]
        return remote(block, block, near_send.at[c], near_recv.at[c], video=partner)

    def far_copy(d, c):
        block = normed.at[video, c]
        return remote(
            block, block, far_send.at[d - 1, c], far_recv.at[d - 1, c], video=video_at(d, core)
        )

    def relay_copy(d, c):
        block = normed.at[video_at(columns - d, core), c]
        return remote(
            block, block, relay_send.at[d - 1, c], relay_recv.at[d - 1, c], video=partner
        )

    for c in range(2):
        part = slice(c * half, (c + 1) * half)
        hidden = (x_ref[part].astype(F32) + convolve(conv_b, c * half, half)).astype(BF16)
        hidden_ref[part] = hidden
        normed[video, c] = layer_norm(hidden.astype(F32)).astype(BF16)
        for d in range(1, columns):
            far_copy(d, c).start()
        near_copy(c).start()
    chain_step(0, 2)
    chain_step(1, 2)
    for i in (8, 9, 10, 11, 13, 14):
        local[i].wait()
    for s in range(2):
        for k in range(3, frames):
            chain_step(s, k)
        chain_step(s + 2, 0)
    chain_finish(0)

    w_key, w_value = matrix(0), matrix(1)

    def project(u):
        both = normed[u].reshape(tokens, channels)
        keys_ref[u] = dot(both, w_key).astype(BF16)
        values_ref[u] = dot(both, w_value).astype(BF16)

    project(video)
    for d in range(1, columns):
        for c in range(2):
            block = normed.at[video_at(columns - d, core), c]
            remote(
                block, block, far_send.at[d - 1, c], far_recv.at[d - 1, c], video=video
            ).wait_recv()
            relay_copy(d, c).start()
        if d == 1:
            for c in range(2):
                block = normed.at[partner, c]
                remote(block, block, near_send.at[c], near_recv.at[c], video=partner).wait_recv()
            project(partner)
        project(video_at(columns - d, core))
    chain_step(2, 1)
    chain_finish(1)
    queries = dot(normed[video].reshape(tokens, channels), matrix(2)).astype(BF16)
    chain_step(3, 1)
    for d in range(1, columns):
        for c in range(2):
            block = normed.at[video_at(columns - d, 1 - core), c]
            remote(
                block, block, relay_send.at[d - 1, c], relay_recv.at[d - 1, c], video=partner
            ).wait_recv()
        project(video_at(columns - d, 1 - core))

    exponent = math.log2(math.e) / math.sqrt(head_width)
    w_out = matrix(3)
    lane_row = iota((1, tokens), 1)
    ones = jnp.ones((tokens, 128), BF16)
    rows_per = tokens // chunks // frames

    def go_copy(c, d):
        to = lax.rem(frame + d, frames)
        return remote(
            send_blocks.at[c, to],
            recv_blocks.at[c, frame],
            go_send.at[c, d - 1],
            go_recv.at[c, d - 1],
            frame=to,
        )

    def ret_copy(c, d):
        to = lax.rem(frame + d, frames)
        return remote(
            back_blocks.at[c, to],
            final_blocks.at[c, frame],
            ret_send.at[c, d - 1],
            ret_recv.at[c, d - 1],
            frame=to,
        )

    def attend(i):
        part = slice(i * half, (i + 1) * half)
        blocks = [jnp.zeros((half, min(128, channels - s)), F32) for s in range(0, channels, 128)]
        for m in range(2):
            target = match_ref[m, video]
            keys = keys_ref[target]
            values = values_ref[target]
            bias_low = jnp.where(mask_ref[m, i, 0, video] > 0, 0.0, FILL)
            bias_high = jnp.where(mask_ref[m, i, 1, video] > 0, 0.0, FILL)
            bias_row = jnp.where(lane_row < half, bias_low, bias_high)
            for h in range(HEADS):
                low = h * head_width // 128 * 128
                high = min(-(-(h + 1) * head_width // 128) * 128, channels)
                lanes = iota((1, high - low), 1) + low
                inside = jnp.logical_and(lanes >= h * head_width, lanes < (h + 1) * head_width)
                inside = jnp.where(inside, 1.0, 0.0).astype(BF16)
                scores = dot_nt(queries[part, low:high] * inside, keys[:, low:high]) + bias_row
                peak = jnp.max(scores, axis=-1, keepdims=True)
                powers = jnp.exp2((scores - peak) * exponent).astype(BF16)
                picked = values[:, low:high] * inside
                if high - low == 128:
                    result = dot(powers, jnp.concatenate([picked, ones], axis=1))
                    total = 1.0 / result[:, 128:]
                else:
                    total = 1.0 / dot(powers, ones)
                    result = dot(powers, picked)
                for s in range(low, high, 128):
                    width = min(128, channels - s)
                    blocks[s // 128] = (
                        blocks[s // 128]
                        + result[:, s - low : s - low + width] * total[:, :width]
                    )
        mixture = jnp.concatenate(blocks, axis=1).astype(BF16)
        second = (hidden_ref[part].astype(F32) + dot(mixture, w_out)).astype(BF16)
        second_ref[part] = second
        return layer_norm(second.astype(F32)).astype(BF16)

    def send_out(c, temp_normed):
        send_blocks[c] = temp_normed.reshape(frames, rows_per, channels)
        for d in range(1, frames):
            go_copy(c, d).start()
        recv_blocks[c, frame] = send_blocks[c, frame]

    if chunks == 2:
        send_out(0, attend(0))
        chain_step(2, 2)
        chain_step(3, 2)
        send_out(1, attend(1))
    else:
        first = attend(0)
        chain_step(2, 2)
        chain_step(3, 2)
        second_part = attend(1)
        send_out(0, jnp.concatenate([first, second_part], axis=0))
    for s in range(2, 4):
        for k in range(3, frames):
            chain_step(s, k)
    chain_finish(2)
    chain_finish(3)

    w_tk, w_tv, w_tq, w_tout = matrix(4), matrix(5), matrix(6), matrix(7)
    lane_head = jnp.floor((iota((channels, 128), 0).astype(F32) + 0.5) / head_width)
    gather_heads = jnp.where(
        lane_head == iota((channels, 128), 1).astype(F32), 1.0, 0.0
    ).astype(BF16)
    row_head = jnp.floor((iota((128, channels), 1).astype(F32) + 0.5) / head_width)
    spread_heads = jnp.where(
        row_head == iota((128, channels), 0).astype(F32), 1.0, 0.0
    ).astype(BF16)

    for c in range(chunks):
        for d in range(1, frames):
            block = recv_blocks.at[c, lax.rem(frame + frames - d, frames)]
            remote(
                block, block, go_send.at[c, d - 1], go_recv.at[c, d - 1], frame=frame
            ).wait_recv()
        stacked = recv_blocks[c].reshape(frames * rows_per, channels)
        q = dot(stacked, w_tq).astype(BF16).astype(F32)
        k = dot(stacked, w_tk).astype(BF16).astype(F32)
        v = dot(stacked, w_tv).astype(BF16).astype(F32)
        for f in range(frames):
            q_f = q[f * rows_per : (f + 1) * rows_per]
            product = jnp.concatenate([q_f] * frames, axis=0) * k
            coarse = product.astype(BF16)
            fine = (product - coarse.astype(F32)).astype(BF16)
            scores = dot(coarse, gather_heads) + dot(fine, gather_heads)
            parts = [scores[g * rows_per : (g + 1) * rows_per] for g in range(frames)]
            peak = functools.reduce(jnp.maximum, parts)
            parts = [jnp.exp2((p - peak) * exponent) for p in parts]
            scale = 1.0 / functools.reduce(jnp.add, parts)
            probs = jnp.concatenate([p * scale for p in parts], axis=0).astype(BF16)
            weighted = dot(probs, spread_heads) * v
            summed = functools.reduce(
                jnp.add, [weighted[g * rows_per : (g + 1) * rows_per] for g in range(frames)]
            )
            back_blocks[c, f] = summed.astype(BF16)
        for d in range(1, frames):
            ret_copy(c, d).start()
        final_blocks[c, frame] = back_blocks[c, frame]

    span = tokens // chunks
    for c in range(chunks):
        for d in range(1, frames):
            block = final_blocks.at[c, lax.rem(frame + frames - d, frames)]
            remote(
                block, block, ret_send.at[c, d - 1], ret_recv.at[c, d - 1], frame=frame
            ).wait_recv()
        part = slice(c * span, (c + 1) * span)
        outcome = final_blocks[c].reshape(span, channels)
        result = second_ref[part].astype(F32) + dot(outcome, w_tout)
        out_ref[0, 0, :, part] = jnp.transpose(result).astype(BF16)

    for d in range(1, frames):
        time_copy(d).wait_send()
        for c in range(chunks):
            go_copy(c, d).wait_send()
            ret_copy(c, d).wait_send()
    for c in range(2):
        near_copy(c).wait_send()
        for d in range(1, columns):
            far_copy(d, c).wait_send()
            relay_copy(d, c).wait_send()
    for s in range(4):
        chain_drain(s)


def per_device(frames, videos, *args):
    (
        latents,
        timesteps,
        matchings,
        tile_mask,
        conv_first,
        conv_second,
        time_proj,
        epi_in,
        epi_out,
        temp_in,
        temp_out,
    ) = args
    tokens, channels = latents.shape[2:]
    rows = epi_out.shape[0]
    columns = videos // 2
    chunks = 2 if (tokens // 2 // frames) % 16 == 0 else 1
    block = (chunks, frames, tokens // chunks // frames, channels)
    dma = pltpu.SemaphoreType.DMA
    hops = max(columns - 1, 1)
    anywhere = pl.BlockSpec(memory_space=pl.ANY)
    result = pl.pallas_call(
        functools.partial(kernel, frames, videos, chunks),
        out_shape=jax.ShapeDtypeStruct((1, 1, channels, tokens), BF16),
        in_specs=[anywhere] * 11,
        out_specs=pl.BlockSpec(memory_space=pltpu.VMEM),
        scratch_shapes=[
            pltpu.SMEM(timesteps.shape, jnp.int32),
            pltpu.SMEM(matchings.shape, jnp.int32),
            pltpu.SMEM((2, 2, 2, tile_mask.shape[1]), jnp.int32),
            pltpu.VMEM((channels, tokens), BF16),
            pltpu.VMEM((tokens, channels), BF16),
            pltpu.VMEM(conv_first.shape, BF16),
            pltpu.VMEM(conv_second.shape, BF16),
            pltpu.VMEM(time_proj.shape, BF16),
            pltpu.VMEM((frames, 8, channels), F32),
            pltpu.VMEM((frames, 8, rows, channels), BF16),
            pltpu.VMEM((3, tokens + 2 * W, channels), BF16),
            pltpu.VMEM((tokens, channels), BF16),
            pltpu.VMEM((videos, 2, tokens // 2, channels), BF16),
            pltpu.VMEM((videos, tokens, channels), BF16),
            pltpu.VMEM((videos, tokens, channels), BF16),
            pltpu.VMEM((tokens, channels), BF16),
            pltpu.VMEM(block, BF16),
            pltpu.VMEM(block, BF16),
            pltpu.VMEM(block, BF16),
            pltpu.VMEM(block, BF16),
            dma((15,)),
            dma((frames,)),
            dma((frames,)),
            dma((4, 2, frames)),
            dma((4, 2, frames)),
            dma((4, 2, frames)),
            dma((4, 2, frames)),
            dma((2,)),
            dma((2,)),
            dma((hops, 2)),
            dma((hops, 2)),
            dma((hops, 2)),
            dma((hops, 2)),
            dma((chunks, frames)),
            dma((chunks, frames)),
            dma((chunks, frames)),
            dma((chunks, frames)),
        ],
        compiler_params=pltpu.CompilerParams(collective_id=0, has_side_effects=True),
    )(
        timesteps,
        matchings,
        jnp.transpose(tile_mask, (0, 2, 3, 1)),
        jnp.swapaxes(latents, 2, 3),
        conv_first,
        conv_second,
        time_proj,
        epi_in,
        epi_out,
        temp_in,
        temp_out,
    )
    return jnp.swapaxes(result, 2, 3)


def solution(mesh):
    placed = (
        P(("groups", "video"), "frame", None, None),
        P(("groups", "video")),
        P(None, "groups"),
        P(None, "groups", None, None),
        P(),
        P(),
        P("frame", None),
        P(None, "frame", None),
        P("frame", None),
        P(None, "frame", None),
        P("frame", None),
    )
    return jax.shard_map(
        functools.partial(per_device, mesh.shape["frame"], mesh.shape["video"]),
        mesh=mesh,
        in_specs=placed,
        out_specs=P(("groups", "video"), "frame", None, None),
        check_vma=False,
    )
```

```python
import functools
import math

import jax
import jax.numpy as jnp
from jax import lax
from jax.experimental import pallas as pl
from jax.experimental.pallas import tpu as pltpu
from jax.sharding import PartitionSpec as P

HEADS = 8
NORM_GROUPS = 32
TEMB = 1280
H = 8
W = 32
EPS = 1e-05
FILL = -1e30
F32 = jnp.float32
BF16 = jnp.bfloat16
MESH = pl.DeviceIdType.MESH


def dot(a, b):
    return jnp.dot(a, b, preferred_element_type=F32)


def dot_nt(a, b):
    return lax.dot_general(a, b, (((1,), (1,)), ((), ())), preferred_element_type=F32)


def iota(shape, dim):
    return lax.broadcasted_iota(jnp.int32, shape, dim)


def split_rows(row):
    hi = row.astype(BF16).astype(F32)
    rest = row - hi
    mid = rest.astype(BF16).astype(F32)
    low = rest - mid
    which = iota((16, row.shape[1]), 0)
    packed = jnp.where(which == 0, hi, jnp.where(which == 1, mid, jnp.where(which == 2, low, 0.0)))
    return packed.astype(BF16)


def group_total(row, same_group):
    return jnp.sum(dot(split_rows(row), same_group), axis=0, keepdims=True)


def gn_silu(values, same_group, count):
    average = group_total(jnp.sum(values, axis=0, keepdims=True), same_group) * (1.0 / count)
    centered = values - average
    spread = group_total(jnp.sum(centered * centered, axis=0, keepdims=True), same_group) * (
        1.0 / count
    )
    u = centered * (1.0 / jnp.sqrt(spread + EPS))
    return u * (1.0 / (1.0 + jnp.exp(-u)))


def layer_norm(values):
    average = jnp.mean(values, axis=-1, keepdims=True)
    centered = values - average
    spread = jnp.mean(centered * centered, axis=-1, keepdims=True)
    return centered * (1.0 / jnp.sqrt(spread + EPS))


def wave(angle, quarter_shift):
    n = jnp.floor(angle * (2.0 / math.pi) + 0.5)
    r = ((angle - n * 1.5703125) - n * 4.837512969970703125e-4) - n * 7.54978995489188216e-8
    z = r * r
    sin_r = r + r * z * (
        -1.6666654611e-1 + z * (8.3321608736e-3 + z * -1.9515295891e-4)
    )
    cos_r = (
        1.0
        - 0.5 * z
        + z * z * (4.166664568298827e-2 + z * (-1.388731625493765e-3 + z * 2.443315711809948e-5))
    )
    q = n + quarter_shift
    q = q - 4.0 * jnp.floor(q * 0.25)
    return jnp.where(
        q < 0.5, cos_r, jnp.where(q < 1.5, -sin_r, jnp.where(q < 2.5, -cos_r, sin_r))
    )


def kernel(
    frames,
    videos,
    chunks,
    steps_hbm,
    match_hbm,
    mask_hbm,
    x_hbm,
    conv_a_hbm,
    conv_b_hbm,
    time_hbm,
    epi_in_hbm,
    epi_out_hbm,
    temp_in_hbm,
    temp_out_hbm,
    out_ref,
    steps_ref,
    match_ref,
    mask_ref,
    xt_ref,
    x_ref,
    conv_a,
    conv_b,
    time_w,
    time_parts,
    weights,
    padded,
    hidden_ref,
    normed,
    keys_ref,
    values_ref,
    second_ref,
    send_blocks,
    recv_blocks,
    back_blocks,
    final_blocks,
    local_sem,
    time_send,
    time_recv,
    chain_send,
    chain_recv,
    pair_send,
    pair_recv,
    near_send,
    near_recv,
    far_send,
    far_recv,
    relay_send,
    relay_recv,
    go_send,
    go_recv,
    ret_send,
    ret_recv,
):
    channels, tokens = xt_ref.shape
    head_width = channels // HEADS
    frame = lax.axis_index("frame")
    video = lax.axis_index("video")
    core = lax.rem(video, 2)
    column = video // 2
    columns = videos // 2
    partner = column * 2 + (1 - core)
    last = frames - 1

    def video_at(shift, which):
        return lax.rem(column + shift, columns) * 2 + which

    barrier = pltpu.get_barrier_semaphore()
    for d in range(1, frames):
        pl.semaphore_signal(
            barrier, inc=1, device_id={"frame": lax.rem(frame + d, frames)}, device_id_type=MESH
        )
    pl.semaphore_signal(barrier, inc=1, device_id={"video": partner}, device_id_type=MESH)
    for d in range(1, columns):
        pl.semaphore_signal(
            barrier, inc=1, device_id={"video": video_at(d, core)}, device_id_type=MESH
        )

    local = [
        (time_hbm, time_w),
        (epi_in_hbm.at[1], weights.at[frame, 0]),
        (epi_in_hbm.at[2], weights.at[frame, 1]),
        (x_hbm.at[0, 0], xt_ref),
        (epi_in_hbm.at[0], weights.at[frame, 2]),
        (epi_out_hbm, weights.at[frame, 3]),
        (conv_a_hbm, conv_a),
        (conv_b_hbm, conv_b),
        (temp_in_hbm.at[1], weights.at[frame, 4]),
        (temp_in_hbm.at[2], weights.at[frame, 5]),
        (temp_in_hbm.at[0], weights.at[frame, 6]),
        (temp_out_hbm, weights.at[frame, 7]),
        (steps_hbm, steps_ref),
        (match_hbm, match_ref),
        (mask_hbm, mask_ref),
    ]
    local = [pltpu.make_async_copy(a, b, local_sem.at[i]) for i, (a, b) in enumerate(local)]
    for i in (12, 0, 3, 1, 2, 4, 5, 6, 7, 8, 9, 10, 11, 13, 14):
        local[i].start()

    def remote(src, dst, send, recv, **where):
        return pltpu.make_async_remote_copy(
            src_ref=src,
            dst_ref=dst,
            send_sem=send,
            recv_sem=recv,
            device_id=where,
            device_id_type=MESH,
        )


    def owner(direction, k):
        return frame - k if direction == 0 else frame + k

    def has(direction, k):
        return frame >= k if direction == 0 else frame + k <= last

    def can_pass(direction):
        return frame < last if direction == 0 else frame > 0

    def chain_copy(s, direction, k):
        block = weights.at[owner(direction, k), s * 2 + core]
        to = frame + 1 if direction == 0 else frame - 1
        return remote(
            block, block, chain_send.at[s, direction, k], chain_recv.at[s, direction, k], frame=to
        )

    def pair_copy(s, direction, k):
        block = weights.at[owner(direction, k), s * 2 + core]
        return remote(
            block, block, pair_send.at[s, direction, k], pair_recv.at[s, direction, k], video=partner
        )

    def chain_step(s, k):
        for direction in range(2):
            if k > 0:

                @pl.when(has(direction, k))
                def _():
                    chain_copy_recv(s, direction, k - 1)
                    pair_copy(s, direction, k).start()

            if k < last:

                @pl.when(jnp.logical_and(has(direction, k), can_pass(direction)))
                def _():
                    chain_copy(s, direction, k).start()

    def chain_copy_recv(s, direction, k):
        block = weights.at[owner(direction, k + 1), s * 2 + core]
        remote(
            block, block, chain_send.at[s, direction, k], chain_recv.at[s, direction, k], frame=frame
        ).wait_recv()

    def chain_finish(s):
        for direction in range(2):
            for k in range(1, frames):

                @pl.when(has(direction, k))
                def _():
                    block = weights.at[owner(direction, k), s * 2 + 1 - core]
                    remote(
                        block,
                        block,
                        pair_send.at[s, direction, k],
                        pair_recv.at[s, direction, k],
                        video=partner,
                    ).wait_recv()

    def chain_drain(s):
        for direction in range(2):
            for k in range(frames):
                if k > 0:

                    @pl.when(has(direction, k))
                    def _():
                        pair_copy(s, direction, k).wait_send()

                if k < last:

                    @pl.when(jnp.logical_and(has(direction, k), can_pass(direction)))
                    def _():
                        chain_copy(s, direction, k).wait_send()

    def matrix(index):
        return jnp.concatenate([weights[f, index] for f in range(frames)], axis=0)

    local[12].wait()
    local[0].wait()
    rows = time_w.shape[0]
    place = iota((16, rows), 1) + frame * rows
    is_sin = place >= TEMB // 2
    index = jnp.where(is_sin, place - TEMB // 2, place).astype(F32)
    frequency = jnp.exp(-math.log(10000.0) * index / (TEMB // 2))
    angle = frequency * steps_ref[0].astype(F32)
    basis = wave(angle, jnp.where(is_sin, 3.0, 0.0))
    time_act = (basis * (1.0 / (1.0 + jnp.exp(-basis)))).astype(BF16)
    time_parts[0] = dot(time_act, time_w[...])[0:8]

    def time_copy(d):
        return remote(
            time_parts.at[0],
            time_parts.at[d],
            time_send.at[d - 1],
            time_recv.at[d - 1],
            frame=lax.rem(frame + d, frames),
        )


    pl.semaphore_wait(barrier, frames + columns - 1)
    for d in range(1, frames):
        time_copy(d).start()
    for i in (1, 2, 4, 5):
        local[i].wait()
    chain_step(0, 0)
    chain_step(1, 0)

    group_width = channels // NORM_GROUPS
    row_group = jnp.floor((iota((channels, channels), 0).astype(F32) + 0.5) / group_width)
    col_group = jnp.floor((iota((channels, channels), 1).astype(F32) + 0.5) / group_width)
    same_group = jnp.where(row_group == col_group, 1.0, 0.0).astype(BF16)
    count = float(tokens * group_width)
    spot = jnp.bitwise_and(iota((tokens, channels), 0), W - 1)
    border = jnp.zeros((W, channels), BF16)
    for side in range(3):
        padded[side, 0:W] = border
        padded[side, W + tokens : W + tokens + W] = border

    def spread_act(act):
        padded[1, W : W + tokens] = act.astype(BF16)
        before = jnp.where(spot == 0, 0.0, pltpu.roll(act, 1, 0))
        padded[0, W : W + tokens] = before.astype(BF16)
        after = jnp.where(spot == W - 1, 0.0, pltpu.roll(act, tokens - 1, 0))
        padded[2, W : W + tokens] = after.astype(BF16)

    def convolve(weight, start, size):
        total = None
        for a in range(3):
            for b in range(3):
                term = dot(padded[b, start + W * a : start + W * a + size], weight[a, b])
                total = term if total is None else total + term
        return total

    local[3].wait()
    source = jnp.transpose(xt_ref[...].astype(F32))
    x_ref[...] = source.astype(BF16)
    spread_act(gn_silu(source, same_group, count))
    local[6].wait()
    inner = convolve(conv_a, 0, tokens)
    channel_mean = jnp.sum(inner, axis=0, keepdims=True) * (1.0 / tokens)
    inner = inner - channel_mean
    channel_spread = jnp.sum(inner * inner, axis=0, keepdims=True)
    chain_step(0, 1)
    bias = time_parts[0, 0:1]
    for d in range(1, frames):
        time_copy(d).wait_recv()
        bias = bias + time_parts[d, 0:1]
    offset = channel_mean + bias
    offset = offset - group_total(offset, same_group) * (1.0 / group_width)
    spread = group_total(channel_spread + tokens * (offset * offset), same_group) * (1.0 / count)
    u = (inner + offset) * (1.0 / jnp.sqrt(spread + EPS))
    spread_act(u * (1.0 / (1.0 + jnp.exp(-u))))
    chain_step(1, 1)
    local[7].wait()
    half = tokens // 2

    def near_copy(c):
        block = normed.at[video, c]
        return remote(block, block, near_send.at[c], near_recv.at[c], video=partner)

    def far_copy(d, c):
        block = normed.at[video, c]
        return remote(
            block, block, far_send.at[d - 1, c], far_recv.at[d - 1, c], video=video_at(d, core)
        )

    def relay_copy(d, c):
        block = normed.at[video_at(columns - d, core), c]
        return remote(
            block, block, relay_send.at[d - 1, c], relay_recv.at[d - 1, c], video=partner
        )

    for c in range(2):
        part = slice(c * half, (c + 1) * half)
        hidden = (x_ref[part].astype(F32) + convolve(conv_b, c * half, half)).astype(BF16)
        hidden_ref[part] = hidden
        normed[video, c] = layer_norm(hidden.astype(F32)).astype(BF16)
        for d in range(1, columns):
            far_copy(d, c).start()
        near_copy(c).start()
    chain_step(0, 2)
    chain_step(1, 2)
    for i in (8, 9, 10, 11, 13, 14):
        local[i].wait()
    for s in range(2):
        for k in range(3, frames):
            chain_step(s, k)
        chain_step(s + 2, 0)
    chain_finish(0)

    w_key, w_value = matrix(0), matrix(1)

    def project(u):
        both = normed[u].reshape(tokens, channels)
        keys_ref[u] = dot(both, w_key).astype(BF16)
        values_ref[u] = dot(both, w_value).astype(BF16)

    project(video)
    for d in range(1, columns):
        for c in range(2):
            block = normed.at[video_at(columns - d, core), c]
            remote(
                block, block, far_send.at[d - 1, c], far_recv.at[d - 1, c], video=video
            ).wait_recv()
            relay_copy(d, c).start()
        if d == 1:
            for c in range(2):
                block = normed.at[partner, c]
                remote(block, block, near_send.at[c], near_recv.at[c], video=partner).wait_recv()
            project(partner)
        project(video_at(columns - d, core))
    chain_step(2, 1)
    chain_finish(1)
    queries = dot(normed[video].reshape(tokens, channels), matrix(2)).astype(BF16)
    chain_step(3, 1)
    for d in range(1, columns):
        for c in range(2):
            block = normed.at[video_at(columns - d, 1 - core), c]
            remote(
                block, block, relay_send.at[d - 1, c], relay_recv.at[d - 1, c], video=partner
            ).wait_recv()
        project(video_at(columns - d, 1 - core))

    exponent = math.log2(math.e) / math.sqrt(head_width)
    w_out = matrix(3)
    lane_row = iota((1, tokens), 1)
    ones = jnp.ones((tokens, 128), BF16)
    rows_per = tokens // chunks // frames

    def go_copy(c, d):
        to = lax.rem(frame + d, frames)
        return remote(
            send_blocks.at[c, to],
            recv_blocks.at[c, frame],
            go_send.at[c, d - 1],
            go_recv.at[c, d - 1],
            frame=to,
        )

    def ret_copy(c, d):
        to = lax.rem(frame + d, frames)
        return remote(
            back_blocks.at[c, to],
            final_blocks.at[c, frame],
            ret_send.at[c, d - 1],
            ret_recv.at[c, d - 1],
            frame=to,
        )

    def attend(i, between=None):
        part = slice(i * half, (i + 1) * half)
        blocks = [jnp.zeros((half, min(128, channels - s)), F32) for s in range(0, channels, 128)]
        for m in range(2):
            if m == 1 and between is not None:
                between()
            target = match_ref[m, video]
            keys = keys_ref[target]
            values = values_ref[target]
            bias_low = jnp.where(mask_ref[m, i, 0, video] > 0, 0.0, FILL)
            bias_high = jnp.where(mask_ref[m, i, 1, video] > 0, 0.0, FILL)
            bias_row = jnp.where(lane_row < half, bias_low, bias_high)
            for h in range(HEADS):
                low = h * head_width // 128 * 128
                high = min(-(-(h + 1) * head_width // 128) * 128, channels)
                lanes = iota((1, high - low), 1) + low
                inside = jnp.logical_and(lanes >= h * head_width, lanes < (h + 1) * head_width)
                inside = jnp.where(inside, 1.0, 0.0).astype(BF16)
                scores = dot_nt(queries[part, low:high] * inside, keys[:, low:high]) + bias_row
                peak = jnp.max(scores, axis=-1, keepdims=True)
                powers = jnp.exp2((scores - peak) * exponent).astype(BF16)
                picked = values[:, low:high] * inside
                if high - low == 128:
                    result = dot(powers, jnp.concatenate([picked, ones], axis=1))
                    total = 1.0 / result[:, 128:]
                else:
                    total = 1.0 / dot(powers, ones)
                    result = dot(powers, picked)
                for s in range(low, high, 128):
                    width = min(128, channels - s)
                    blocks[s // 128] = (
                        blocks[s // 128]
                        + result[:, s - low : s - low + width] * total[:, :width]
                    )
        mixture = jnp.concatenate(blocks, axis=1).astype(BF16)
        second = (hidden_ref[part].astype(F32) + dot(mixture, w_out)).astype(BF16)
        second_ref[part] = second
        return layer_norm(second.astype(F32)).astype(BF16)

    def send_out(c, temp_normed):
        send_blocks[c] = temp_normed.reshape(frames, rows_per, channels)
        for d in range(1, frames):
            go_copy(c, d).start()
        recv_blocks[c, frame] = send_blocks[c, frame]

    def late_hop():
        chain_step(2, 2)
        chain_step(3, 2)

    if chunks == 2:
        send_out(0, attend(0, late_hop))
        if frames > 3:
            chain_step(2, 3)
            chain_step(3, 3)
        send_out(1, attend(1))
    else:
        first = attend(0, late_hop)
        if frames > 3:
            chain_step(2, 3)
            chain_step(3, 3)
        second_part = attend(1)
        send_out(0, jnp.concatenate([first, second_part], axis=0))
    for s in range(2, 4):
        for k in range(4, frames):
            chain_step(s, k)
    chain_finish(2)
    chain_finish(3)

    w_tk, w_tv, w_tq, w_tout = matrix(4), matrix(5), matrix(6), matrix(7)
    lane_head = jnp.floor((iota((channels, 128), 0).astype(F32) + 0.5) / head_width)
    gather_heads = jnp.where(
        lane_head == iota((channels, 128), 1).astype(F32), 1.0, 0.0
    ).astype(BF16)
    row_head = jnp.floor((iota((128, channels), 1).astype(F32) + 0.5) / head_width)
    spread_heads = jnp.where(
        row_head == iota((128, channels), 0).astype(F32), 1.0, 0.0
    ).astype(BF16)

    for c in range(chunks):
        for d in range(1, frames):
            block = recv_blocks.at[c, lax.rem(frame + frames - d, frames)]
            remote(
                block, block, go_send.at[c, d - 1], go_recv.at[c, d - 1], frame=frame
            ).wait_recv()
        stacked = recv_blocks[c].reshape(frames * rows_per, channels)
        q = dot(stacked, w_tq).astype(BF16).astype(F32)
        k = dot(stacked, w_tk).astype(BF16).astype(F32)
        v = dot(stacked, w_tv).astype(BF16).astype(F32)
        for f in range(frames):
            q_f = q[f * rows_per : (f + 1) * rows_per]
            product = jnp.concatenate([q_f] * frames, axis=0) * k
            coarse = product.astype(BF16)
            fine = (product - coarse.astype(F32)).astype(BF16)
            scores = dot(coarse, gather_heads) + dot(fine, gather_heads)
            parts = [scores[g * rows_per : (g + 1) * rows_per] for g in range(frames)]
            peak = functools.reduce(jnp.maximum, parts)
            parts = [jnp.exp2((p - peak) * exponent) for p in parts]
            scale = 1.0 / functools.reduce(jnp.add, parts)
            probs = jnp.concatenate([p * scale for p in parts], axis=0).astype(BF16)
            weighted = dot(probs, spread_heads) * v
            summed = functools.reduce(
                jnp.add, [weighted[g * rows_per : (g + 1) * rows_per] for g in range(frames)]
            )
            back_blocks[c, f] = summed.astype(BF16)
        for d in range(1, frames):
            ret_copy(c, d).start()
        final_blocks[c, frame] = back_blocks[c, frame]

    span = tokens // chunks
    for c in range(chunks):
        for d in range(1, frames):
            block = final_blocks.at[c, lax.rem(frame + frames - d, frames)]
            remote(
                block, block, ret_send.at[c, d - 1], ret_recv.at[c, d - 1], frame=frame
            ).wait_recv()
        part = slice(c * span, (c + 1) * span)
        outcome = final_blocks[c].reshape(span, channels)
        result = second_ref[part].astype(F32) + dot(outcome, w_tout)
        out_ref[0, 0, :, part] = jnp.transpose(result).astype(BF16)

    for d in range(1, frames):
        time_copy(d).wait_send()
        for c in range(chunks):
            go_copy(c, d).wait_send()
            ret_copy(c, d).wait_send()
    for c in range(2):
        near_copy(c).wait_send()
        for d in range(1, columns):
            far_copy(d, c).wait_send()
            relay_copy(d, c).wait_send()
    for s in range(4):
        chain_drain(s)


def per_device(frames, videos, *args):
    (
        latents,
        timesteps,
        matchings,
        tile_mask,
        conv_first,
        conv_second,
        time_proj,
        epi_in,
        epi_out,
        temp_in,
        temp_out,
    ) = args
    tokens, channels = latents.shape[2:]
    rows = epi_out.shape[0]
    columns = videos // 2
    chunks = 2 if (tokens // 2 // frames) % 16 == 0 else 1
    block = (chunks, frames, tokens // chunks // frames, channels)
    dma = pltpu.SemaphoreType.DMA
    hops = max(columns - 1, 1)
    anywhere = pl.BlockSpec(memory_space=pl.ANY)
    result = pl.pallas_call(
        functools.partial(kernel, frames, videos, chunks),
        out_shape=jax.ShapeDtypeStruct((1, 1, channels, tokens), BF16),
        in_specs=[anywhere] * 11,
        out_specs=pl.BlockSpec(memory_space=pltpu.VMEM),
        scratch_shapes=[
            pltpu.SMEM(timesteps.shape, jnp.int32),
            pltpu.SMEM(matchings.shape, jnp.int32),
            pltpu.SMEM((2, 2, 2, tile_mask.shape[1]), jnp.int32),
            pltpu.VMEM((channels, tokens), BF16),
            pltpu.VMEM((tokens, channels), BF16),
            pltpu.VMEM(conv_first.shape, BF16),
            pltpu.VMEM(conv_second.shape, BF16),
            pltpu.VMEM(time_proj.shape, BF16),
            pltpu.VMEM((frames, 8, channels), F32),
            pltpu.VMEM((frames, 8, rows, channels), BF16),
            pltpu.VMEM((3, tokens + 2 * W, channels), BF16),
            pltpu.VMEM((tokens, channels), BF16),
            pltpu.VMEM((videos, 2, tokens // 2, channels), BF16),
            pltpu.VMEM((videos, tokens, channels), BF16),
            pltpu.VMEM((videos, tokens, channels), BF16),
            pltpu.VMEM((tokens, channels), BF16),
            pltpu.VMEM(block, BF16),
            pltpu.VMEM(block, BF16),
            pltpu.VMEM(block, BF16),
            pltpu.VMEM(block, BF16),
            dma((15,)),
            dma((frames,)),
            dma((frames,)),
            dma((4, 2, frames)),
            dma((4, 2, frames)),
            dma((4, 2, frames)),
            dma((4, 2, frames)),
            dma((2,)),
            dma((2,)),
            dma((hops, 2)),
            dma((hops, 2)),
            dma((hops, 2)),
            dma((hops, 2)),
            dma((chunks, frames)),
            dma((chunks, frames)),
            dma((chunks, frames)),
            dma((chunks, frames)),
        ],
        compiler_params=pltpu.CompilerParams(collective_id=0, has_side_effects=True),
    )(
        timesteps,
        matchings,
        jnp.transpose(tile_mask, (0, 2, 3, 1)),
        jnp.swapaxes(latents, 2, 3),
        conv_first,
        conv_second,
        time_proj,
        epi_in,
        epi_out,
        temp_in,
        temp_out,
    )
    return jnp.swapaxes(result, 2, 3)


def solution(mesh):
    placed = (
        P(("groups", "video"), "frame", None, None),
        P(("groups", "video")),
        P(None, "groups"),
        P(None, "groups", None, None),
        P(),
        P(),
        P("frame", None),
        P(None, "frame", None),
        P("frame", None),
        P(None, "frame", None),
        P("frame", None),
    )
    return jax.shard_map(
        functools.partial(per_device, mesh.shape["frame"], mesh.shape["video"]),
        mesh=mesh,
        in_specs=placed,
        out_specs=P(("groups", "video"), "frame", None, None),
        check_vma=False,
    )
```

```python
import functools
import math

import jax
import jax.numpy as jnp
from jax import lax
from jax.experimental import pallas as pl
from jax.experimental.pallas import tpu as pltpu
from jax.sharding import PartitionSpec as P

HEADS = 8
NORM_GROUPS = 32
TEMB = 1280
H = 8
W = 32
EPS = 1e-05
FILL = -1e30
F32 = jnp.float32
BF16 = jnp.bfloat16
MESH = pl.DeviceIdType.MESH


def dot(a, b):
    return jnp.dot(a, b, preferred_element_type=F32)


def dot_nt(a, b):
    return lax.dot_general(a, b, (((1,), (1,)), ((), ())), preferred_element_type=F32)


def iota(shape, dim):
    return lax.broadcasted_iota(jnp.int32, shape, dim)


def split_rows(row):
    hi = row.astype(BF16).astype(F32)
    rest = row - hi
    mid = rest.astype(BF16).astype(F32)
    low = rest - mid
    which = iota((16, row.shape[1]), 0)
    packed = jnp.where(which == 0, hi, jnp.where(which == 1, mid, jnp.where(which == 2, low, 0.0)))
    return packed.astype(BF16)


def group_total(row, same_group):
    return jnp.sum(dot(split_rows(row), same_group), axis=0, keepdims=True)


def gn_silu(values, same_group, count):
    average = group_total(jnp.sum(values, axis=0, keepdims=True), same_group) * (1.0 / count)
    centered = values - average
    spread = group_total(jnp.sum(centered * centered, axis=0, keepdims=True), same_group) * (
        1.0 / count
    )
    u = centered * (1.0 / jnp.sqrt(spread + EPS))
    return u * (1.0 / (1.0 + jnp.exp(-u)))


def layer_norm(values):
    average = jnp.mean(values, axis=-1, keepdims=True)
    centered = values - average
    spread = jnp.mean(centered * centered, axis=-1, keepdims=True)
    return centered * (1.0 / jnp.sqrt(spread + EPS))


def wave(angle, quarter_shift):
    n = jnp.floor(angle * (2.0 / math.pi) + 0.5)
    r = ((angle - n * 1.5703125) - n * 4.837512969970703125e-4) - n * 7.54978995489188216e-8
    z = r * r
    sin_r = r + r * z * (
        -1.6666654611e-1 + z * (8.3321608736e-3 + z * -1.9515295891e-4)
    )
    cos_r = (
        1.0
        - 0.5 * z
        + z * z * (4.166664568298827e-2 + z * (-1.388731625493765e-3 + z * 2.443315711809948e-5))
    )
    q = n + quarter_shift
    q = q - 4.0 * jnp.floor(q * 0.25)
    return jnp.where(
        q < 0.5, cos_r, jnp.where(q < 1.5, -sin_r, jnp.where(q < 2.5, -cos_r, sin_r))
    )


def kernel(
    frames,
    videos,
    chunks,
    steps_hbm,
    match_hbm,
    mask_hbm,
    x_hbm,
    conv_a_hbm,
    conv_b_hbm,
    time_hbm,
    epi_in_hbm,
    epi_out_hbm,
    temp_in_hbm,
    temp_out_hbm,
    out_ref,
    steps_ref,
    match_ref,
    mask_ref,
    xt_ref,
    x_ref,
    conv_a,
    conv_b,
    time_w,
    time_parts,
    weights,
    padded,
    hidden_ref,
    normed,
    keys_ref,
    values_ref,
    second_ref,
    send_blocks,
    recv_blocks,
    back_blocks,
    final_blocks,
    local_sem,
    time_send,
    time_recv,
    chain_send,
    chain_recv,
    pair_send,
    pair_recv,
    near_send,
    near_recv,
    far_send,
    far_recv,
    relay_send,
    relay_recv,
    go_send,
    go_recv,
    ret_send,
    ret_recv,
):
    channels, tokens = xt_ref.shape
    head_width = channels // HEADS
    frame = lax.axis_index("frame")
    video = lax.axis_index("video")
    core = lax.rem(video, 2)
    column = video // 2
    columns = videos // 2
    partner = column * 2 + (1 - core)
    last = frames - 1

    def video_at(shift, which):
        return lax.rem(column + shift, columns) * 2 + which

    barrier = pltpu.get_barrier_semaphore()
    for d in range(1, frames):
        pl.semaphore_signal(
            barrier, inc=1, device_id={"frame": lax.rem(frame + d, frames)}, device_id_type=MESH
        )
    pl.semaphore_signal(barrier, inc=1, device_id={"video": partner}, device_id_type=MESH)
    for d in range(1, columns):
        pl.semaphore_signal(
            barrier, inc=1, device_id={"video": video_at(d, core)}, device_id_type=MESH
        )

    local = [
        (time_hbm, time_w),
        (epi_in_hbm.at[1], weights.at[frame, 0]),
        (epi_in_hbm.at[2], weights.at[frame, 1]),
        (x_hbm.at[0, 0], xt_ref),
        (epi_in_hbm.at[0], weights.at[frame, 2]),
        (epi_out_hbm, weights.at[frame, 3]),
        (conv_a_hbm, conv_a),
        (conv_b_hbm, conv_b),
        (temp_in_hbm.at[1], weights.at[frame, 4]),
        (temp_in_hbm.at[2], weights.at[frame, 5]),
        (temp_in_hbm.at[0], weights.at[frame, 6]),
        (temp_out_hbm, weights.at[frame, 7]),
        (steps_hbm, steps_ref),
        (match_hbm, match_ref),
        (mask_hbm, mask_ref),
    ]
    local = [pltpu.make_async_copy(a, b, local_sem.at[i]) for i, (a, b) in enumerate(local)]
    for i in (12, 0, 3, 1, 2, 4, 5, 6, 7, 8, 9, 10, 11, 13, 14):
        local[i].start()

    def remote(src, dst, send, recv, **where):
        return pltpu.make_async_remote_copy(
            src_ref=src,
            dst_ref=dst,
            send_sem=send,
            recv_sem=recv,
            device_id=where,
            device_id_type=MESH,
        )


    def owner(direction, k):
        return frame - k if direction == 0 else frame + k

    def has(direction, k):
        return frame >= k if direction == 0 else frame + k <= last

    def can_pass(direction):
        return frame < last if direction == 0 else frame > 0

    def chain_copy(s, direction, k):
        block = weights.at[owner(direction, k), s * 2 + core]
        to = frame + 1 if direction == 0 else frame - 1
        return remote(
            block, block, chain_send.at[s, direction, k], chain_recv.at[s, direction, k], frame=to
        )

    def pair_copy(s, direction, k):
        block = weights.at[owner(direction, k), s * 2 + core]
        return remote(
            block, block, pair_send.at[s, direction, k], pair_recv.at[s, direction, k], video=partner
        )

    def chain_step(s, k):
        for direction in range(2):
            if k > 0:

                @pl.when(has(direction, k))
                def _():
                    chain_copy_recv(s, direction, k - 1)
                    pair_copy(s, direction, k).start()

            if k < last:

                @pl.when(jnp.logical_and(has(direction, k), can_pass(direction)))
                def _():
                    chain_copy(s, direction, k).start()

    def chain_copy_recv(s, direction, k):
        block = weights.at[owner(direction, k + 1), s * 2 + core]
        remote(
            block, block, chain_send.at[s, direction, k], chain_recv.at[s, direction, k], frame=frame
        ).wait_recv()

    def chain_finish(s):
        for direction in range(2):
            for k in range(1, frames):

                @pl.when(has(direction, k))
                def _():
                    block = weights.at[owner(direction, k), s * 2 + 1 - core]
                    remote(
                        block,
                        block,
                        pair_send.at[s, direction, k],
                        pair_recv.at[s, direction, k],
                        video=partner,
                    ).wait_recv()

    def chain_drain(s):
        for direction in range(2):
            for k in range(frames):
                if k > 0:

                    @pl.when(has(direction, k))
                    def _():
                        pair_copy(s, direction, k).wait_send()

                if k < last:

                    @pl.when(jnp.logical_and(has(direction, k), can_pass(direction)))
                    def _():
                        chain_copy(s, direction, k).wait_send()

    def matrix(index):
        return jnp.concatenate([weights[f, index] for f in range(frames)], axis=0)

    local[12].wait()
    local[0].wait()
    rows = time_w.shape[0]
    place = iota((16, rows), 1) + frame * rows
    is_sin = place >= TEMB // 2
    index = jnp.where(is_sin, place - TEMB // 2, place).astype(F32)
    frequency = jnp.exp(-math.log(10000.0) * index / (TEMB // 2))
    angle = frequency * steps_ref[0].astype(F32)
    basis = wave(angle, jnp.where(is_sin, 3.0, 0.0))
    time_act = (basis * (1.0 / (1.0 + jnp.exp(-basis)))).astype(BF16)
    time_parts[0] = dot(time_act, time_w[...])[0:8]

    def time_copy(d):
        return remote(
            time_parts.at[0],
            time_parts.at[d],
            time_send.at[d - 1],
            time_recv.at[d - 1],
            frame=lax.rem(frame + d, frames),
        )


    group_width = channels // NORM_GROUPS
    row_group = jnp.floor((iota((channels, channels), 0).astype(F32) + 0.5) / group_width)
    col_group = jnp.floor((iota((channels, channels), 1).astype(F32) + 0.5) / group_width)
    same_group = jnp.where(row_group == col_group, 1.0, 0.0).astype(BF16)
    count = float(tokens * group_width)
    spot = jnp.bitwise_and(iota((tokens, channels), 0), W - 1)
    border = jnp.zeros((W, channels), BF16)
    for side in range(3):
        padded[side, 0:W] = border
        padded[side, W + tokens : W + tokens + W] = border

    def spread_act(act):
        padded[1, W : W + tokens] = act.astype(BF16)
        before = jnp.where(spot == 0, 0.0, pltpu.roll(act, 1, 0))
        padded[0, W : W + tokens] = before.astype(BF16)
        after = jnp.where(spot == W - 1, 0.0, pltpu.roll(act, tokens - 1, 0))
        padded[2, W : W + tokens] = after.astype(BF16)

    def convolve(weight, start, size):
        total = None
        for a in range(3):
            for b in range(3):
                term = dot(padded[b, start + W * a : start + W * a + size], weight[a, b])
                total = term if total is None else total + term
        return total

    local[3].wait()
    source = jnp.transpose(xt_ref[...].astype(F32))
    x_ref[...] = source.astype(BF16)
    spread_act(gn_silu(source, same_group, count))
    pl.semaphore_wait(barrier, frames + columns - 1)
    for d in range(1, frames):
        time_copy(d).start()
    for i in (1, 2, 4, 5):
        local[i].wait()
    chain_step(0, 0)
    chain_step(1, 0)
    local[6].wait()
    inner = convolve(conv_a, 0, tokens)
    channel_mean = jnp.sum(inner, axis=0, keepdims=True) * (1.0 / tokens)
    inner = inner - channel_mean
    channel_spread = jnp.sum(inner * inner, axis=0, keepdims=True)
    chain_step(0, 1)
    bias = time_parts[0, 0:1]
    for d in range(1, frames):
        time_copy(d).wait_recv()
        bias = bias + time_parts[d, 0:1]
    offset = channel_mean + bias
    offset = offset - group_total(offset, same_group) * (1.0 / group_width)
    spread = group_total(channel_spread + tokens * (offset * offset), same_group) * (1.0 / count)
    u = (inner + offset) * (1.0 / jnp.sqrt(spread + EPS))
    spread_act(u * (1.0 / (1.0 + jnp.exp(-u))))
    chain_step(1, 1)
    local[7].wait()
    half = tokens // 2

    def near_copy(c):
        block = normed.at[video, c]
        return remote(block, block, near_send.at[c], near_recv.at[c], video=partner)

    def far_copy(d, c):
        block = normed.at[video, c]
        return remote(
            block, block, far_send.at[d - 1, c], far_recv.at[d - 1, c], video=video_at(d, core)
        )

    def relay_copy(d, c):
        block = normed.at[video_at(columns - d, core), c]
        return remote(
            block, block, relay_send.at[d - 1, c], relay_recv.at[d - 1, c], video=partner
        )

    for c in range(2):
        part = slice(c * half, (c + 1) * half)
        hidden = (x_ref[part].astype(F32) + convolve(conv_b, c * half, half)).astype(BF16)
        hidden_ref[part] = hidden
        normed[video, c] = layer_norm(hidden.astype(F32)).astype(BF16)
        for d in range(1, columns):
            far_copy(d, c).start()
        near_copy(c).start()
        chain_step(c, 2)
    for i in (8, 9, 10, 11, 13, 14):
        local[i].wait()
    for s in range(2):
        for k in range(3, frames):
            chain_step(s, k)
        chain_step(s + 2, 0)
    chain_finish(0)

    w_key, w_value = matrix(0), matrix(1)

    def project(u):
        both = normed[u].reshape(tokens, channels)
        keys_ref[u] = dot(both, w_key).astype(BF16)
        values_ref[u] = dot(both, w_value).astype(BF16)

    project(video)
    for d in range(1, columns):
        for c in range(2):
            block = normed.at[video_at(columns - d, core), c]
            remote(
                block, block, far_send.at[d - 1, c], far_recv.at[d - 1, c], video=video
            ).wait_recv()
            relay_copy(d, c).start()
        if d == 1:
            for c in range(2):
                block = normed.at[partner, c]
                remote(block, block, near_send.at[c], near_recv.at[c], video=partner).wait_recv()
            project(partner)
        project(video_at(columns - d, core))
    chain_step(2, 1)
    chain_finish(1)
    queries = dot(normed[video].reshape(tokens, channels), matrix(2)).astype(BF16)
    chain_step(3, 1)
    for d in range(1, columns):
        for c in range(2):
            block = normed.at[video_at(columns - d, 1 - core), c]
            remote(
                block, block, relay_send.at[d - 1, c], relay_recv.at[d - 1, c], video=partner
            ).wait_recv()
        project(video_at(columns - d, 1 - core))

    exponent = math.log2(math.e) / math.sqrt(head_width)
    w_out = matrix(3)
    lane_row = iota((1, tokens), 1)
    ones = jnp.ones((tokens, 128), BF16)
    rows_per = tokens // chunks // frames

    def go_copy(c, d):
        to = lax.rem(frame + d, frames)
        return remote(
            send_blocks.at[c, to],
            recv_blocks.at[c, frame],
            go_send.at[c, d - 1],
            go_recv.at[c, d - 1],
            frame=to,
        )

    def ret_copy(c, d):
        to = lax.rem(frame + d, frames)
        return remote(
            back_blocks.at[c, to],
            final_blocks.at[c, frame],
            ret_send.at[c, d - 1],
            ret_recv.at[c, d - 1],
            frame=to,
        )

    def attend(i, between=None):
        part = slice(i * half, (i + 1) * half)
        blocks = [jnp.zeros((half, min(128, channels - s)), F32) for s in range(0, channels, 128)]
        for m in range(2):
            if m == 1 and between is not None:
                between()
            target = match_ref[m, video]
            keys = keys_ref[target]
            values = values_ref[target]
            bias_low = jnp.where(mask_ref[m, i, 0, video] > 0, 0.0, FILL)
            bias_high = jnp.where(mask_ref[m, i, 1, video] > 0, 0.0, FILL)
            bias_row = jnp.where(lane_row < half, bias_low, bias_high)
            for h in range(HEADS):
                low = h * head_width // 128 * 128
                high = min(-(-(h + 1) * head_width // 128) * 128, channels)
                lanes = iota((1, high - low), 1) + low
                inside = jnp.logical_and(lanes >= h * head_width, lanes < (h + 1) * head_width)
                inside = jnp.where(inside, 1.0, 0.0).astype(BF16)
                scores = dot_nt(queries[part, low:high] * inside, keys[:, low:high]) + bias_row
                peak = jnp.max(scores, axis=-1, keepdims=True)
                powers = jnp.exp2((scores - peak) * exponent).astype(BF16)
                picked = values[:, low:high] * inside
                if high - low == 128:
                    result = dot(powers, jnp.concatenate([picked, ones], axis=1))
                    total = 1.0 / result[:, 128:]
                else:
                    total = 1.0 / dot(powers, ones)
                    result = dot(powers, picked)
                for s in range(low, high, 128):
                    width = min(128, channels - s)
                    blocks[s // 128] = (
                        blocks[s // 128]
                        + result[:, s - low : s - low + width] * total[:, :width]
                    )
        mixture = jnp.concatenate(blocks, axis=1).astype(BF16)
        second = (hidden_ref[part].astype(F32) + dot(mixture, w_out)).astype(BF16)
        second_ref[part] = second
        return layer_norm(second.astype(F32)).astype(BF16)

    def send_out(c, temp_normed):
        send_blocks[c] = temp_normed.reshape(frames, rows_per, channels)
        for d in range(1, frames):
            go_copy(c, d).start()
        recv_blocks[c, frame] = send_blocks[c, frame]

    def late_hop():
        chain_step(2, 2)
        chain_step(3, 2)

    if chunks == 2:
        send_out(0, attend(0))
        late_hop()
        send_out(1, attend(1))
    else:
        first = attend(0, late_hop)
        if frames > 3:
            chain_step(2, 3)
            chain_step(3, 3)
        second_part = attend(1)
        send_out(0, jnp.concatenate([first, second_part], axis=0))
    for s in range(2, 4):
        for k in range(3, frames):
            chain_step(s, k)
    chain_finish(2)
    chain_finish(3)

    w_tk, w_tv, w_tq, w_tout = matrix(4), matrix(5), matrix(6), matrix(7)
    lane_head = jnp.floor((iota((channels, 128), 0).astype(F32) + 0.5) / head_width)
    gather_heads = jnp.where(
        lane_head == iota((channels, 128), 1).astype(F32), 1.0, 0.0
    ).astype(BF16)
    row_head = jnp.floor((iota((128, channels), 1).astype(F32) + 0.5) / head_width)
    spread_heads = jnp.where(
        row_head == iota((128, channels), 0).astype(F32), 1.0, 0.0
    ).astype(BF16)

    for c in range(chunks):
        for d in range(1, frames):
            block = recv_blocks.at[c, lax.rem(frame + frames - d, frames)]
            remote(
                block, block, go_send.at[c, d - 1], go_recv.at[c, d - 1], frame=frame
            ).wait_recv()
        stacked = recv_blocks[c].reshape(frames * rows_per, channels)
        q = dot(stacked, w_tq).astype(BF16).astype(F32)
        k = dot(stacked, w_tk).astype(BF16).astype(F32)
        v = dot(stacked, w_tv).astype(BF16).astype(F32)
        for f in range(frames):
            q_f = q[f * rows_per : (f + 1) * rows_per]
            product = jnp.concatenate([q_f] * frames, axis=0) * k
            coarse = product.astype(BF16)
            fine = (product - coarse.astype(F32)).astype(BF16)
            scores = dot(coarse, gather_heads) + dot(fine, gather_heads)
            parts = [scores[g * rows_per : (g + 1) * rows_per] for g in range(frames)]
            peak = functools.reduce(jnp.maximum, parts)
            parts = [jnp.exp2((p - peak) * exponent) for p in parts]
            scale = 1.0 / functools.reduce(jnp.add, parts)
            probs = jnp.concatenate([p * scale for p in parts], axis=0).astype(BF16)
            weighted = dot(probs, spread_heads) * v
            summed = functools.reduce(
                jnp.add, [weighted[g * rows_per : (g + 1) * rows_per] for g in range(frames)]
            )
            back_blocks[c, f] = summed.astype(BF16)
        for d in range(1, frames):
            ret_copy(c, d).start()
        final_blocks[c, frame] = back_blocks[c, frame]

    span = tokens // chunks
    for c in range(chunks):
        for d in range(1, frames):
            block = final_blocks.at[c, lax.rem(frame + frames - d, frames)]
            remote(
                block, block, ret_send.at[c, d - 1], ret_recv.at[c, d - 1], frame=frame
            ).wait_recv()
        part = slice(c * span, (c + 1) * span)
        outcome = final_blocks[c].reshape(span, channels)
        result = second_ref[part].astype(F32) + dot(outcome, w_tout)
        out_ref[0, 0, :, part] = jnp.transpose(result).astype(BF16)

    for d in range(1, frames):
        time_copy(d).wait_send()
        for c in range(chunks):
            go_copy(c, d).wait_send()
            ret_copy(c, d).wait_send()
    for c in range(2):
        near_copy(c).wait_send()
        for d in range(1, columns):
            far_copy(d, c).wait_send()
            relay_copy(d, c).wait_send()
    for s in range(4):
        chain_drain(s)


def per_device(frames, videos, *args):
    (
        latents,
        timesteps,
        matchings,
        tile_mask,
        conv_first,
        conv_second,
        time_proj,
        epi_in,
        epi_out,
        temp_in,
        temp_out,
    ) = args
    tokens, channels = latents.shape[2:]
    rows = epi_out.shape[0]
    columns = videos // 2
    chunks = 2 if (tokens // 2 // frames) % 16 == 0 else 1
    block = (chunks, frames, tokens // chunks // frames, channels)
    dma = pltpu.SemaphoreType.DMA
    hops = max(columns - 1, 1)
    anywhere = pl.BlockSpec(memory_space=pl.ANY)
    result = pl.pallas_call(
        functools.partial(kernel, frames, videos, chunks),
        out_shape=jax.ShapeDtypeStruct((1, 1, channels, tokens), BF16),
        in_specs=[anywhere] * 11,
        out_specs=pl.BlockSpec(memory_space=pltpu.VMEM),
        scratch_shapes=[
            pltpu.SMEM(timesteps.shape, jnp.int32),
            pltpu.SMEM(matchings.shape, jnp.int32),
            pltpu.SMEM((2, 2, 2, tile_mask.shape[1]), jnp.int32),
            pltpu.VMEM((channels, tokens), BF16),
            pltpu.VMEM((tokens, channels), BF16),
            pltpu.VMEM(conv_first.shape, BF16),
            pltpu.VMEM(conv_second.shape, BF16),
            pltpu.VMEM(time_proj.shape, BF16),
            pltpu.VMEM((frames, 8, channels), F32),
            pltpu.VMEM((frames, 8, rows, channels), BF16),
            pltpu.VMEM((3, tokens + 2 * W, channels), BF16),
            pltpu.VMEM((tokens, channels), BF16),
            pltpu.VMEM((videos, 2, tokens // 2, channels), BF16),
            pltpu.VMEM((videos, tokens, channels), BF16),
            pltpu.VMEM((videos, tokens, channels), BF16),
            pltpu.VMEM((tokens, channels), BF16),
            pltpu.VMEM(block, BF16),
            pltpu.VMEM(block, BF16),
            pltpu.VMEM(block, BF16),
            pltpu.VMEM(block, BF16),
            dma((15,)),
            dma((frames,)),
            dma((frames,)),
            dma((4, 2, frames)),
            dma((4, 2, frames)),
            dma((4, 2, frames)),
            dma((4, 2, frames)),
            dma((2,)),
            dma((2,)),
            dma((hops, 2)),
            dma((hops, 2)),
            dma((hops, 2)),
            dma((hops, 2)),
            dma((chunks, frames)),
            dma((chunks, frames)),
            dma((chunks, frames)),
            dma((chunks, frames)),
        ],
        compiler_params=pltpu.CompilerParams(collective_id=0, has_side_effects=True),
    )(
        timesteps,
        matchings,
        jnp.transpose(tile_mask, (0, 2, 3, 1)),
        jnp.swapaxes(latents, 2, 3),
        conv_first,
        conv_second,
        time_proj,
        epi_in,
        epi_out,
        temp_in,
        temp_out,
    )
    return jnp.swapaxes(result, 2, 3)


def solution(mesh):
    placed = (
        P(("groups", "video"), "frame", None, None),
        P(("groups", "video")),
        P(None, "groups"),
        P(None, "groups", None, None),
        P(),
        P(),
        P("frame", None),
        P(None, "frame", None),
        P("frame", None),
        P(None, "frame", None),
        P("frame", None),
    )
    return jax.shard_map(
        functools.partial(per_device, mesh.shape["frame"], mesh.shape["video"]),
        mesh=mesh,
        in_specs=placed,
        out_specs=P(("groups", "video"), "frame", None, None),
        check_vma=False,
    )
```
